32 devices in a mesh: grp: 2 (over y), seq: 4 (over z), sub: 4 (over x, core).
Axes of the slice: x: 2, y: 2, z: 4, core: 2. Of those that a mesh axis runs over, the one named last changes fastest.
Arguments:
- activations: bfloat16 [32768, 384], P(('grp', 'seq', 'sub')), parts along dimension 0, may hold values from -6 to 6
- cotangent: bfloat16 [32768, 384], P(('grp', 'seq', 'sub')), parts along dimension 0, may hold values from -6 to 6
- weights: bfloat16 [2304, 384], P('sub'), may hold values from -0.1875 to 0.1875
Outputs:
- input_grad: bfloat16 [32768, 384], P(('grp', 'seq', 'sub')), parts along dimension 0
- weight_grad: float32 [4608, 384], P(('grp', 'sub')), parts along dimension 0
The draws below stay inside these ranges and needn't reach their ends.
There are 2 independent parts, one for each index of `grp`. The reference program is written for one: setup_inputs(seed, part) draws one part's arguments, and reference() takes and returns one part's arrays. A program takes and returns all parts, laid end to end along the dimension named above; an argument that names none is the same for every part. Nothing has to cross between parts.
All inputs are finite; a program needn't handle non-finite values.
Results may differ from the reference program's by a relative error of at most 0.0053.
Values may be sent and summed in bfloat16 or wider, within the bound.
No kernel may reach another device: no remote copies, remote signals or barrier semaphores. Data moves between devices by JAX's collectives and lax.ppermute only.
A program may use at most 64 MiB of HBM per device.

```python
import math
import jax
import jax.numpy as jnp

C = 384
DILATION_FIRST = 1024
DILATION_SECOND = 2048
POSITIONS = 16384


def spiked(result, own_key, source, target, blocks, factor):
    def block_of(dim):
        return (jnp.arange(result.shape[dim]) // (result.shape[dim] // blocks)).reshape((-1,) + (1,) * (result.ndim - 1 - dim))

    near = jax.random.permutation(own_key, blocks)[block_of(target)]
    far = (block_of(target) + blocks // 2) % blocks
    return jnp.where((block_of(source) == near) | (block_of(source) == far), factor * result, result)


def shard_levels(own_key, dims, pieces, smallest, high):
    gain = 1.0
    for position, blocks in pieces:
        steps = jax.random.uniform(jax.random.fold_in(jax.random.fold_in(own_key, 6), position), (blocks,), jnp.float32, smallest / len(pieces), high / len(pieces))
        gain = gain * jnp.repeat(jnp.exp(steps), dims[position] // blocks).reshape((-1,) + (1,) * (len(dims) - 1 - position))
    return gain


def bell_draw(stream_key, shape, deviation, bound, shards=(), held_as=jnp.bfloat16):
    level = shard_levels(stream_key, shape, shards, -0.22, 0.18) if shards else 1.0
    entries = jax.random.normal(stream_key, shape, jnp.float32) * deviation * level
    return jnp.minimum(jnp.maximum(entries, -bound), bound).astype(held_as)


def noise_with(own_key, dims, deviation, most, shards, heavy, kind=jnp.bfloat16):
    result = deviation * jax.random.normal(own_key, dims, jnp.float32)
    if shards:
        result = result * shard_levels(own_key, dims, shards, -0.22, 0.18)
    return jnp.clip(spiked(result, jax.random.fold_in(own_key, 3), *heavy), -most, most).astype(kind)


def setup_inputs(seed: int = 0, part: int = 0) -> dict:
    streams_of = jax.random.split(jax.random.key(seed), 4)
    own_keys = jax.random.split(jax.random.fold_in(streams_of[3], part), 4)
    activations = noise_with(own_keys[0], (POSITIONS, C), 1.0, 6.0, ((0, 16),), (0, 1, 16, 2.0))
    cotangent = bell_draw(own_keys[1], (POSITIONS, C), 1.0, 6.0, ((0, 16),))
    weights = bell_draw(streams_of[2], (6 * C, C), (3 * C) ** -0.5, 0.1875, ((0, 4),))
    return dict(activations=activations, cotangent=cotangent, weights=weights)


def gelu_pair(pre_act):
    coeff = 0.7978845608
    tanh_value = jnp.tanh(coeff * (pre_act + 0.044715 * pre_act * pre_act * pre_act))
    gelu_value = 0.5 * pre_act * (1.0 + tanh_value)
    gelu_slope = 0.5 * (1.0 + tanh_value) + 0.5 * pre_act * (1.0 - tanh_value * tanh_value) * coeff * (1.0 + 3.0 * 0.044715 * pre_act * pre_act)
    return (gelu_value, gelu_slope)

def backward_shifted(source, distance):
    empty = jnp.zeros((distance, source.shape[1]), source.dtype)
    return jnp.concatenate((empty, source[:-distance]), 0)

def forward_shifted(source, distance):
    empty = jnp.zeros((distance, source.shape[1]), source.dtype)
    return jnp.concatenate((source[distance:], empty), 0)

def back_matrix(kernel):
    return kernel.reshape(3, C, C).transpose(0, 2, 1).reshape(3 * C, C)

def reference(activations, cotangent, weights):
    first = weights[:3 * C]
    second = weights[3 * C:]
    first_layer_weights = jnp.concatenate((backward_shifted(activations, DILATION_FIRST), activations, forward_shifted(activations, DILATION_FIRST)), 1)
    pre_one = jnp.dot(first_layer_weights, first, preferred_element_type=jnp.float32)
    gelu_one, slope_one = gelu_pair(pre_one)
    middle_state = (activations.astype(jnp.float32) + gelu_one).astype(jnp.bfloat16)
    second_layer_weights = jnp.concatenate((backward_shifted(middle_state, DILATION_SECOND), middle_state, forward_shifted(middle_state, DILATION_SECOND)), 1)
    pre_two = jnp.dot(second_layer_weights, second, preferred_element_type=jnp.float32)
    gelu_two, slope_two = gelu_pair(pre_two)
    second_error = (cotangent.astype(jnp.float32) * slope_two).astype(jnp.bfloat16)
    grad_scale = 1.0 / math.sqrt(POSITIONS)
    grad_two = jnp.dot(second_layer_weights.T, second_error, preferred_element_type=jnp.float32) * grad_scale
    second_reach = jnp.concatenate((forward_shifted(second_error, DILATION_SECOND), second_error, backward_shifted(second_error, DILATION_SECOND)), 1)
    back_one = cotangent.astype(jnp.float32) + jnp.dot(second_reach, back_matrix(second), preferred_element_type=jnp.float32)
    first_error = (back_one * slope_one).astype(jnp.bfloat16)
    grad_one = jnp.dot(first_layer_weights.T, first_error, preferred_element_type=jnp.float32) * grad_scale
    first_reach = jnp.concatenate((forward_shifted(first_error, DILATION_FIRST), first_error, backward_shifted(first_error, DILATION_FIRST)), 1)
    input_grad = (back_one + jnp.dot(first_reach, back_matrix(first), preferred_element_type=jnp.float32)).astype(jnp.bfloat16)
    return (input_grad, jnp.concatenate((grad_one, grad_two), 0))
```

```python
import math

import jax
import jax.numpy as jnp
from jax import lax
from jax.sharding import PartitionSpec as P

DILATION_FIRST = 1024
DILATION_SECOND = 2048
F32 = jnp.float32
BF16 = jnp.bfloat16


def shift_route(axis, distance):
    n = lax.axis_size(axis)
    return [(i, i + distance) for i in range(n) if 0 <= i + distance < n]


def xor_swap(block, axis, bits):
    n = lax.axis_size(axis)
    return lax.ppermute(block, axis, [(i, i ^ bits) for i in range(n)])


def by_xor(pieces, j):
    bit = 1
    while bit < len(pieces):
        flip = (j & bit) != 0
        pieces = [jnp.where(flip, pieces[r ^ bit], pieces[r]) for r in range(len(pieces))]
        bit *= 2
    return pieces


def exchange(block, axis):
    n = lax.axis_size(axis)
    j = lax.axis_index(axis)
    rows = block.shape[0] // n
    pieces = [lax.dynamic_slice_in_dim(block, (j ^ r) * rows, rows, 0) for r in range(n)]
    got = [pieces[0]] + [xor_swap(pieces[r], axis, r) for r in range(1, n)]
    return jnp.concatenate(by_xor(got, j), 0)


def gather_rows(block, axis):
    n = lax.axis_size(axis)
    j = lax.axis_index(axis)
    held = [block]
    bit = n // 2
    order = [0]
    while bit:
        held = held + [xor_swap(b, axis, bit) for b in held]
        order = order + [o ^ bit for o in order]
        bit //= 2
    pieces = [held[order.index(r)] for r in range(n)]
    return jnp.concatenate(by_xor(pieces, j), 0)


def gelu_pair(pre_act):
    coeff = 0.7978845608
    tanh_value = jnp.tanh(coeff * (pre_act + 0.044715 * pre_act * pre_act * pre_act))
    gelu_value = 0.5 * pre_act * (1.0 + tanh_value)
    gelu_slope = 0.5 * (1.0 + tanh_value) + 0.5 * pre_act * (
        1.0 - tanh_value * tanh_value
    ) * coeff * (1.0 + 3.0 * 0.044715 * pre_act * pre_act)
    return (gelu_value, gelu_slope)


def tap_stack(ext, step, rows):
    return jnp.concatenate([ext[k * step : k * step + rows] for k in range(3)], 1)


def back_product(spread, kernel):
    channels = kernel.shape[1]
    spread_three = spread.reshape(spread.shape[0], 3, channels)
    kernel_three = kernel.reshape(3, channels, channels)
    return lax.dot_general(
        spread_three, kernel_three, (((1, 2), (0, 2)), ((), ())), preferred_element_type=F32
    )


def tap_grads(stacked, delta):
    return lax.dot_general(stacked, delta, (((0,), (0,)), ((), ())), preferred_element_type=F32)


def halo(block, rows):
    low = lax.ppermute(block[block.shape[0] - rows :], "seq", shift_route("seq", 1))
    high = lax.ppermute(block[:rows], "seq", shift_route("seq", -1))
    return low, high


def sum_over_sub(grad, low_owner):
    n = lax.axis_size("sub")
    j = lax.axis_index("sub")
    owners = n // 2
    parts = grad.reshape(owners, -1, grad.shape[1])
    bit = 1
    kept = parts
    while bit < n:
        mine = (j & bit) != 0
        if kept.shape[0] > 1:
            even, odd = kept[0::2], kept[1::2]
            keep = jnp.where(mine, odd, even)
            send = jnp.where(mine, even, odd)
            wire = F32 if bit == 1 else BF16
            kept = keep + xor_swap(send.astype(wire), "sub", bit).astype(F32)
        else:
            to_high = low_owner > 0
            route = [(i, i ^ bit) for i in range(n) if ((i & bit) == 0) == to_high]
            kept = kept + lax.ppermute(kept.astype(BF16), "sub", route).astype(F32)
        bit *= 2
    return kept[0]


def sum_over_seq(part):
    n = lax.axis_size("seq")
    if n > 4:
        return lax.psum(part, "seq")
    sent = part.astype(BF16)
    total = part
    for turn in range(1, n):
        route = [(i, (i + turn) % n) for i in range(n)]
        total = total + lax.ppermute(sent, "seq", route).astype(F32)
    return total


def per_device(activations, cotangent, weights):
    count_of_rows, channels = activations.shape
    groups, members = lax.axis_size("seq"), lax.axis_size("sub")
    s = lax.axis_index("seq")
    j = lax.axis_index("sub")
    near = DILATION_FIRST // count_of_rows
    far = DILATION_SECOND // count_of_rows
    q = count_of_rows // members
    grad_scale = 1.0 / math.sqrt(count_of_rows * groups * members)

    act = exchange(activations, "sub")
    act_low, act_high = halo(act, (near + far) * q)
    all_weights = gather_rows(weights, "sub")
    first = all_weights[: 3 * channels]
    second = all_weights[3 * channels :]
    cot = exchange(cotangent, "sub")
    cot_low, cot_high = halo(cot, near * q)
    cot_ext = jnp.concatenate((cot_low, cot, cot_high), 0)

    def inside(margin):
        place = lax.broadcasted_iota(jnp.int32, (count_of_rows + 2 * margin * q, 1), 0)
        low_ok = (s > 0) | (place >= margin * q)
        high_ok = (s < groups - 1) | (place < count_of_rows + margin * q)
        return low_ok & high_ok

    act_ext = jnp.concatenate((act_low, act, act_high), 0)
    wide = count_of_rows + 2 * far * q
    act_stack = tap_stack(act_ext, near * q, wide)
    pre_one = jnp.dot(act_stack, first, preferred_element_type=F32)
    gelu_one, slope_one = gelu_pair(pre_one)
    hidden = (act_ext[near * q : near * q + wide].astype(F32) + gelu_one).astype(BF16)
    hidden = jnp.where(inside(far), hidden, jnp.zeros_like(hidden))
    hid_stack = tap_stack(hidden, far * q, count_of_rows)
    pre_two = jnp.dot(hid_stack, second, preferred_element_type=F32)
    _, slope_two = gelu_pair(pre_two)
    delta_two = (cot.astype(F32) * slope_two).astype(BF16)

    two_low, two_high = halo(delta_two, (near + far) * q)
    grad_two = tap_grads(hid_stack, delta_two) * grad_scale
    part_two = sum_over_sub(grad_two, members // 2)

    two_ext = jnp.concatenate((two_low, delta_two, two_high), 0)
    mid = count_of_rows + 2 * near * q
    two_spread = jnp.concatenate(
        [two_ext[k * far * q : k * far * q + mid] for k in (2, 1, 0)], 1
    )
    back_one = cot_ext.astype(F32) + back_product(two_spread, second)
    skip = (far - near) * q
    delta_one = (back_one * slope_one[skip : skip + mid]).astype(BF16)
    delta_one = jnp.where(inside(near), delta_one, jnp.zeros_like(delta_one))
    own_one = delta_one[near * q : near * q + count_of_rows]
    own_stack = act_stack[far * q : far * q + count_of_rows]
    grad_one = tap_grads(own_stack, own_one) * grad_scale
    part_one = sum_over_sub(grad_one, 0)
    one_spread = jnp.concatenate(
        [delta_one[k * near * q : k * near * q + count_of_rows] for k in (2, 1, 0)], 1
    )
    grad_in = back_one[near * q : near * q + count_of_rows] + back_product(one_spread, first)
    input_grad = exchange(grad_in.astype(BF16), "sub")

    part = jnp.where(j >= members // 2, part_two, part_one)
    weight_grad = sum_over_seq(part)
    return (input_grad, weight_grad)


def solution(mesh):
    placed = (P(("grp", "seq", "sub"), None), P(("grp", "seq", "sub"), None), P("sub", None))
    return jax.shard_map(
        per_device,
        mesh=mesh,
        in_specs=placed,
        out_specs=(P(("grp", "seq", "sub"), None), P(("grp", "sub"), None)),
        check_vma=False,
    )
```

```python
import functools
import math

import jax
import jax.numpy as jnp
from jax import lax
from jax.experimental import pallas as pl
from jax.experimental.pallas import tpu as pltpu
from jax.sharding import PartitionSpec as P

DILATION_FIRST = 1024
DILATION_SECOND = 2048
F32 = jnp.float32
BF16 = jnp.bfloat16
SMEM = pl.BlockSpec(memory_space=pltpu.SMEM)
VMEM = pl.BlockSpec(memory_space=pltpu.VMEM)


def shifted(block, axis, distance):
    n = lax.axis_size(axis)
    route = [(i, i + distance) for i in range(n) if 0 <= i + distance < n]
    return lax.ppermute(block, axis, route)


def turned(block, axis, turn):
    n = lax.axis_size(axis)
    return lax.ppermute(block, axis, [(i, (i + turn) % n) for i in range(n)])


def swapped(block, axis, bits):
    n = lax.axis_size(axis)
    return lax.ppermute(block, axis, [(i, i ^ bits) for i in range(n)])


def after(value, *others):
    return lax.optimization_barrier((value,) + others)[0]


def cut(block, index, rows):
    return lax.dynamic_slice_in_dim(block, index * rows, rows, 0)


def gather_pieces(block, axis, others):
    n = lax.axis_size(axis)
    held = {0: block}
    bit = n // 2
    while bit:
        for r in list(held):
            first_far = r == 0 and bit == n // 2
            source = after(held[r], others) if first_far else held[r]
            held[r ^ bit] = swapped(source, axis, bit)
        bit //= 2
    return [held[r] for r in range(n)]


def slope_of(v, th):
    coeff = 0.7978845608
    return 0.5 * (1.0 + th) + 0.5 * v * (1.0 - th * th) * coeff * (1.0 + 3.0 * 0.044715 * v * v)


def gelu_tanh(v):
    coeff = 0.7978845608
    return jnp.tanh(coeff * (v + 0.044715 * v * v * v))


def dot(a, b):
    return jnp.dot(a, b, preferred_element_type=F32)


def forward_kernel(sizes, place, *refs):
    groups, members, q, near, far = sizes
    own_e, own_l, low_e, low_l, high_e, high_l = refs[:6]
    w_pieces = refs[6 : 6 + members]
    c_pieces = refs[6 + members : 6 + 2 * members]
    outs = refs[6 + 2 * members :]
    act_stack, hid_stack, slope_one, delta, to_high, to_low, cot_out, w_out = outs[:8]
    ext, hid = outs[8:]
    s, j = place[0], place[1]
    rows = w_pieces[0].shape[0]
    for r in range(members):
        at = j ^ r
        for side, (early, late) in enumerate(((low_e, low_l), (own_e, own_l), (high_e, high_l))):
            source = early[r * q : (r + 1) * q] if r < 2 else late[(r - 2) * q : (r - 1) * q]
            ext[side * members + at] = source
        w_out[pl.ds(pl.multiple_of(at * rows, 16), rows), :] = w_pieces[r][...]
        cot_out[pl.ds(pl.multiple_of(at * q, 16), q), :] = c_pieces[r][...]
    taps = w_out.shape[0] // 2
    for b in range(-far, members + far):
        k = members + b
        stack = jnp.concatenate([ext[k - near], ext[k], ext[k + near]], 1)
        pre = dot(stack, w_out[:taps])
        th = gelu_tanh(pre)
        value = (ext[k].astype(F32) + 0.5 * pre * (1.0 + th)).astype(BF16)
        if b < 0:
            value = jnp.where(s > 0, value, jnp.zeros_like(value))
        if b >= members:
            value = jnp.where(s < groups - 1, value, jnp.zeros_like(value))
        hid[b + far] = value
        if 0 <= b < members:
            slope_one[b * q : (b + 1) * q] = slope_of(pre, th)
            act_stack[b * q : (b + 1) * q] = stack
    for b in range(members):
        stack = jnp.concatenate([hid[b], hid[b + far], hid[b + 2 * far]], 1)
        here = slice(b * q, (b + 1) * q)
        hid_stack[here] = stack
        pre = dot(stack, w_out[taps:])
        value = (cot_out[here].astype(F32) * slope_of(pre, gelu_tanh(pre))).astype(BF16)
        delta[here] = value
        if b < far:
            to_low[here] = value
        if b >= members - far:
            at = b - (members - far)
            to_high[at * q : (at + 1) * q] = value


def back_kernel(sizes, low, own, high, cot, slope, w_back, back_one, delta, to_high, to_low):
    members, q, near, far = sizes

    def block(b):
        if b < 0:
            return low[(b + far) * q : (b + far + 1) * q]
        if b >= members:
            return high[(b - members) * q : (b - members + 1) * q]
        return own[b * q : (b + 1) * q]

    for b in range(members):
        here = slice(b * q, (b + 1) * q)
        stack = jnp.concatenate([block(b + far), block(b), block(b - far)], 1)
        back = cot[here].astype(F32) + dot(stack, w_back[...])
        back_one[here] = back
        value = (back * slope[here]).astype(BF16)
        delta[here] = value
        if b < near:
            to_low[here] = value
        if b >= members - near:
            at = b - (members - near)
            to_high[at * q : (at + 1) * q] = value


def input_kernel(sizes, place, low, own, high, back_one, w_back, out):
    members, q, near = sizes
    j = place[1]

    def block(b):
        if b < 0:
            return low[(b + near) * q : (b + near + 1) * q]
        if b >= members:
            return high[(b - members) * q : (b - members + 1) * q]
        return own[b * q : (b + 1) * q]

    for b in range(members):
        here = slice(b * q, (b + 1) * q)
        stack = jnp.concatenate([block(b + near), block(b), block(b - near)], 1)
        value = (back_one[here] + dot(stack, w_back[...])).astype(BF16)
        out[pl.ds(pl.multiple_of((j ^ b) * q, 16), q), :] = value


def call(kernel, out_shapes, scratch=(), scalars=0, operands=()):
    specs = [SMEM] * scalars + [VMEM] * (len(operands) - scalars)
    return pl.pallas_call(
        kernel,
        out_shape=tuple(jax.ShapeDtypeStruct(shape, kind) for shape, kind in out_shapes),
        in_specs=specs,
        out_specs=tuple(VMEM for _ in out_shapes),
        scratch_shapes=list(scratch),
        compiler_params=pltpu.CompilerParams(vmem_limit_bytes=48 * 1024 * 1024),
    )(*operands)


def tap_grads(stacked, delta):
    return lax.dot_general(stacked, delta, (((0,), (0,)), ((), ())), preferred_element_type=F32)


def core_stage(grad, j):
    owners = lax.axis_size("sub") // 2
    parts = grad.reshape(owners, -1, grad.shape[1])
    odd = (j & 1) != 0
    keep = jnp.where(odd, parts[1::2], parts[0::2])
    send = jnp.where(odd, parts[0::2], parts[1::2])
    return keep + swapped(send, "sub", 1)


def seq_stage(part, s):
    n = lax.axis_size("seq")
    if n > 4:
        return lax.psum(part, "seq")
    rows = part.shape[1] // n

    def share(index):
        return lax.dynamic_slice_in_dim(part, index * rows, rows, 1)

    total = share(s)
    for turn in range(1, n):
        piece = share(lax.rem(s + turn, n)).astype(BF16)
        total = total + turned(piece, "seq", turn).astype(F32)
    return total


def chip_stage(part, j, high_layer):
    n = lax.axis_size("sub")
    bit = 2
    while bit < n:
        if part.shape[0] > 1:
            mine = (j & bit) != 0
            keep = jnp.where(mine, part[1::2], part[0::2])
            send = jnp.where(mine, part[0::2], part[1::2])
            part = keep + swapped(send.astype(BF16), "sub", bit).astype(F32)
        else:
            route = [(i, i ^ bit) for i in range(n) if ((i & bit) == 0) == high_layer]
            part = part + lax.ppermute(part.astype(BF16), "sub", route).astype(F32)
        bit *= 2
    return part[0]


def spread_seq(total, s):
    n = lax.axis_size("seq")
    if n > 4:
        return total
    rows, channels = total.shape
    whole = jnp.zeros((n * rows, channels), F32)
    whole = lax.dynamic_update_slice_in_dim(whole, total, s * rows, 0)
    sent = total.astype(BF16)
    for turn in range(1, n):
        got = turned(sent, "seq", turn).astype(F32)
        whole = lax.dynamic_update_slice_in_dim(whole, got, lax.rem(s + n - turn, n) * rows, 0)
    return whole


def per_device(activations, cotangent, weights):
    count, channels = activations.shape
    groups, members = lax.axis_size("seq"), lax.axis_size("sub")
    s, j = lax.axis_index("seq"), lax.axis_index("sub")
    place = jnp.stack([s, j]).astype(jnp.int32)
    near, far = DILATION_FIRST // count, DILATION_SECOND // count
    q = count // members
    taps = 3 * channels
    grad_scale = 1.0 / math.sqrt(count * groups * members)

    pieces = [cut(activations, j ^ r, q) for r in range(members)]
    got = [pieces[0]] + [swapped(pieces[r], "sub", r) for r in range(1, members)]
    own_e = jnp.concatenate(got[:2], 0)
    low_e, high_e = shifted(own_e, "seq", 1), shifted(own_e, "seq", -1)
    own_l = jnp.concatenate(got[2:], 0)
    low_l, high_l = shifted(own_l, "seq", 1), shifted(own_l, "seq", -1)

    w_pieces = gather_pieces(weights, "sub", own_l)
    c_cut = [cut(cotangent, j ^ r, q) for r in range(members)]
    far_weights = w_pieces[members // 2]
    c_pieces = c_cut[:1] + [
        swapped(after(c_cut[r], far_weights) if r > 1 else c_cut[r], "sub", r)
        for r in range(1, members)
    ]

    act_stack, hid_stack, slope_one, delta_two, up_two, down_two, cot, all_weights = call(
        functools.partial(forward_kernel, (groups, members, q, near, far)),
        (
            ((count, taps), BF16),
            ((count, taps), BF16),
            ((count, channels), F32),
            ((count, channels), BF16),
            ((far * q, channels), BF16),
            ((far * q, channels), BF16),
            ((count, channels), BF16),
            ((2 * taps, channels), BF16),
        ),
        (
            pltpu.VMEM((3 * members, q, channels), BF16),
            pltpu.VMEM((members + 2 * far, q, channels), BF16),
        ),
        1,
        (place, own_e, own_l, low_e, low_l, high_e, high_l, *w_pieces, *c_pieces),
    )
    two_low, two_high = shifted(up_two, "seq", 1), shifted(down_two, "seq", -1)
    back = all_weights.reshape(2, 3, channels, channels).transpose(0, 1, 3, 2)
    back = back.reshape(2, taps, channels)
    back_first, back_second = back[0], back[1]

    grad_two = tap_grads(hid_stack, delta_two) * grad_scale
    part_two = chip_stage(seq_stage(core_stage(grad_two, j), s), j, True)

    back_one, delta_one, up_one, down_one = call(
        functools.partial(back_kernel, (members, q, near, far)),
        (
            ((count, channels), F32),
            ((count, channels), BF16),
            ((near * q, channels), BF16),
            ((near * q, channels), BF16),
        ),
        operands=(two_low, delta_two, two_high, cot, slope_one, back_second),
    )
    one_low, one_high = shifted(up_one, "seq", 1), shifted(down_one, "seq", -1)
    grad_one = tap_grads(act_stack, delta_one) * grad_scale
    part_one = chip_stage(seq_stage(core_stage(grad_one, j), s), j, False)

    (grad_in,) = call(
        functools.partial(input_kernel, (members, q, near)),
        (((count, channels), BF16),),
        scalars=1,
        operands=(place, one_low, delta_one, one_high, back_one, back_first),
    )
    input_grad = jnp.zeros((count, channels), BF16)
    for r in range(members):
        piece = grad_in[r * q : (r + 1) * q]
        piece = swapped(piece, "sub", r) if r else piece
        input_grad = lax.dynamic_update_slice_in_dim(input_grad, piece, (j ^ r) * q, 0)

    weight_grad = spread_seq(jnp.where(j >= members // 2, part_two, part_one), s)
    return (input_grad, weight_grad)


def solution(mesh):
    placed = (P(("grp", "seq", "sub"), None), P(("grp", "seq", "sub"), None), P("sub", None))
    return jax.shard_map(
        per_device,
        mesh=mesh,
        in_specs=placed,
        out_specs=(P(("grp", "seq", "sub"), None), P(("grp", "sub"), None)),
        check_vma=False,
    )
```

```python
import functools
import math

import jax
import jax.numpy as jnp
from jax import lax
from jax.experimental import pallas as pl
from jax.experimental.pallas import tpu as pltpu
from jax.sharding import PartitionSpec as P

DILATION_FIRST = 1024
DILATION_SECOND = 2048
F32 = jnp.float32
BF16 = jnp.bfloat16
SMEM = pl.BlockSpec(memory_space=pltpu.SMEM)
VMEM = pl.BlockSpec(memory_space=pltpu.VMEM)


def shifted(block, axis, distance):
    n = lax.axis_size(axis)
    route = [(i, i + distance) for i in range(n) if 0 <= i + distance < n]
    return lax.ppermute(block, axis, route)


def turned(block, axis, turn):
    n = lax.axis_size(axis)
    return lax.ppermute(block, axis, [(i, (i + turn) % n) for i in range(n)])


def swapped(block, axis, bits):
    n = lax.axis_size(axis)
    return lax.ppermute(block, axis, [(i, i ^ bits) for i in range(n)])


def after(value, others):
    return lax.optimization_barrier((value, others))[0]


def cut(block, index, rows):
    return lax.dynamic_slice_in_dim(block, index * rows, rows, 0)


def gather_pieces(block, axis, others):
    n = lax.axis_size(axis)
    held = {0: block}
    bit = n // 2
    while bit:
        for r in list(held):
            first_far = r == 0 and bit == n // 2
            source = after(held[r], others) if first_far else held[r]
            held[r ^ bit] = swapped(source, axis, bit)
        bit //= 2
    return [held[r] for r in range(n)]


def slope_of(v, th):
    coeff = 0.7978845608
    return 0.5 * (1.0 + th) + 0.5 * v * (1.0 - th * th) * coeff * (1.0 + 3.0 * 0.044715 * v * v)


def gelu_tanh(v):
    coeff = 0.7978845608
    return jnp.tanh(coeff * (v + 0.044715 * v * v * v))


def dot(a, b):
    return jnp.dot(a, b, preferred_element_type=F32)


def back_dot(blocks, w, first):
    channels = w.shape[1]
    total = None
    for k, block in enumerate(blocks):
        tap = w[first + k * channels : first + (k + 1) * channels]
        part = lax.dot_general(block, tap, (((1,), (1,)), ((), ())), preferred_element_type=F32)
        total = part if total is None else total + part
    return total


def regroup_kernel(sizes, place, block, *refs):
    members, q, reach = sizes
    pieces, (own, to_high, to_low) = refs[: members - 1], refs[members - 1 :]
    j = place[1]

    def rows(index):
        return pl.ds(pl.multiple_of(index * q, 16), q)

    own[rows(j), :] = block[rows(j), :]
    for r in range(1, members):
        own[rows(j ^ r), :] = pieces[r - 1][...]
    to_high[...] = own[(members - reach) * q :]
    to_low[...] = own[: reach * q]


def forward_kernel(sizes, place, low, own, high, *refs):
    groups, members, q, near, far = sizes
    w_pieces, (act_stack, hid_stack, slope_one, slope_two, w_out, hid) = (
        refs[:members],
        refs[members:],
    )
    s, j = place[0], place[1]
    reach = near + far
    rows = w_pieces[0].shape[0]
    for r in range(members):
        w_out[pl.ds(pl.multiple_of((j ^ r) * rows, 16), rows), :] = w_pieces[r][...]
    taps = w_out.shape[0] // 2

    def block(b):
        if b < 0:
            return low[(b + reach) * q : (b + reach + 1) * q]
        if b >= members:
            return high[(b - members) * q : (b - members + 1) * q]
        return own[b * q : (b + 1) * q]

    for b in range(-far, members + far):
        stack = jnp.concatenate([block(b - near), block(b), block(b + near)], 1)
        pre = dot(stack, w_out[:taps])
        th = gelu_tanh(pre)
        value = (block(b).astype(F32) + 0.5 * pre * (1.0 + th)).astype(BF16)
        if b < 0:
            value = jnp.where(s > 0, value, jnp.zeros_like(value))
        if b >= members:
            value = jnp.where(s < groups - 1, value, jnp.zeros_like(value))
        hid[b + far] = value
        if 0 <= b < members:
            slope_one[b * q : (b + 1) * q] = slope_of(pre, th)
            act_stack[b * q : (b + 1) * q] = stack
    for b in range(members):
        stack = jnp.concatenate([hid[b], hid[b + far], hid[b + 2 * far]], 1)
        here = slice(b * q, (b + 1) * q)
        hid_stack[here] = stack
        pre = dot(stack, w_out[taps:])
        slope_two[here] = slope_of(pre, gelu_tanh(pre))


def delta_kernel(sizes, place, slope, cotangent, *refs):
    members, q, far = sizes
    pieces, (delta, to_high, to_low, cot) = refs[: members - 1], refs[members - 1 :]
    j = place[1]

    def rows(index):
        return pl.ds(pl.multiple_of(index * q, 16), q)

    cot[rows(j), :] = cotangent[rows(j), :]
    for r in range(1, members):
        cot[rows(j ^ r), :] = pieces[r - 1][...]
    for b in range(members):
        here = slice(b * q, (b + 1) * q)
        delta[here] = (cot[here].astype(F32) * slope[here]).astype(BF16)
    to_high[...] = delta[(members - far) * q :]
    to_low[...] = delta[: far * q]


def grad_kernel(sizes, scale, place, stack, delta, *refs):
    members, halo = sizes
    keep, send = refs[-2:] if not halo else refs[-4:-2]
    odd = place[1] & 1
    channels = delta.shape[1]
    rows = 3 * channels // (members // 2)
    for k in range(3):
        first = k * channels
        part = scale * lax.dot_general(
            stack[:, first : first + channels],
            delta[...],
            (((0,), (0,)), ((), ())),
            preferred_element_type=F32,
        )
        for owner in range(members // 2):
            start, stop = max(first, owner * rows), min(first + channels, (owner + 1) * rows)
            if start >= stop:
                continue
            at = (owner // 2) * rows + start - owner * rows
            value = part[start - first : stop - first]

            @pl.when(odd == owner % 2)
            def _():
                keep[at : at + stop - start] = value

            @pl.when(odd != owner % 2)
            def _():
                send[at : at + stop - start] = value

    if halo:
        to_high, to_low = refs[-2:]
        to_high[...] = delta[delta.shape[0] - halo :]
        to_low[...] = delta[:halo]


def share_kernel(n, place, keep, other, *refs):
    outs = refs[-n:]
    rows = outs[0].shape[0]
    for turn in range(n):
        at = pl.ds(pl.multiple_of(lax.rem(place[0] + turn, n) * rows, 16), rows)
        outs[turn][...] = (keep[at, :] + other[at, :]).astype(outs[turn].dtype)


def back_kernel(sizes, low, own, high, cot, slope, w, back_one, delta):
    members, q, near, far = sizes

    def block(b):
        if b < 0:
            return low[(b + far) * q : (b + far + 1) * q]
        if b >= members:
            return high[(b - members) * q : (b - members + 1) * q]
        return own[b * q : (b + 1) * q]

    for b in range(members):
        here = slice(b * q, (b + 1) * q)
        product = back_dot((block(b + far), block(b), block(b - far)), w, w.shape[0] // 2)
        back = cot[here].astype(F32) + product
        back_one[here] = back
        delta[here] = (back * slope[here]).astype(BF16)


def input_kernel(sizes, place, low, own, high, back_one, w, out):
    members, q, near = sizes
    j = place[1]

    def block(b):
        if b < 0:
            return low[(b + near) * q : (b + near + 1) * q]
        if b >= members:
            return high[(b - members) * q : (b - members + 1) * q]
        return own[b * q : (b + 1) * q]

    for b in range(members):
        here = slice(b * q, (b + 1) * q)
        product = back_dot((block(b + near), block(b), block(b - near)), w, 0)
        value = (back_one[here] + product).astype(BF16)
        out[pl.ds(pl.multiple_of((j ^ b) * q, 16), q), :] = value


def call(kernel, out_shapes, scratch=(), scalars=0, operands=()):
    specs = [SMEM] * scalars + [VMEM] * (len(operands) - scalars)
    return pl.pallas_call(
        kernel,
        out_shape=tuple(jax.ShapeDtypeStruct(shape, kind) for shape, kind in out_shapes),
        in_specs=specs,
        out_specs=tuple(VMEM for _ in out_shapes),
        scratch_shapes=list(scratch),
        cost_estimate=pl.CostEstimate(flops=1, transcendentals=0, bytes_accessed=1),
        compiler_params=pltpu.CompilerParams(vmem_limit_bytes=16 * 1024 * 1024),
    )(*operands)


def seq_shares(place, keep, other, waits):
    n = lax.axis_size("seq")
    if n > 4:
        return [keep + other]
    shape = (keep.shape[0] // n, keep.shape[1])
    return call(
        functools.partial(share_kernel, n),
        ((shape, F32),) + ((shape, BF16),) * (n - 1),
        scalars=1,
        operands=(place, keep, other, *waits),
    )


def seq_sum(shares):
    if len(shares) == 1:
        return lax.psum(shares[0], "seq")
    total = shares[0]
    for turn in range(1, len(shares)):
        total = total + turned(shares[turn], "seq", turn).astype(F32)
    return total


def chip_sum(total_one, total_two, j):
    n = lax.axis_size("sub")
    owned = n // 4
    one = total_one.reshape(owned, -1, total_one.shape[1])
    two = total_two.reshape(owned, -1, total_two.shape[1])
    high = j >= n // 2
    part, send = jnp.where(high, two, one), jnp.where(high, one, two)
    part = part + swapped(send.astype(BF16), "sub", n // 2).astype(F32)
    bit = 2
    while bit < n // 2:
        mine = (j & bit) != 0
        keep, send = jnp.where(mine, part[1::2], part[0::2]), jnp.where(mine, part[0::2], part[1::2])
        part = keep + swapped(send.astype(BF16), "sub", bit).astype(F32)
        bit *= 2
    return part[0]


def spread_seq(total, sent, s):
    n = lax.axis_size("seq")
    if n > 4:
        return total
    rows, channels = total.shape
    whole = jnp.zeros((n * rows, channels), F32)
    whole = lax.dynamic_update_slice_in_dim(whole, total, s * rows, 0)
    for turn in range(1, n):
        got = turned(sent, "seq", turn).astype(F32)
        whole = lax.dynamic_update_slice_in_dim(whole, got, lax.rem(s + n - turn, n) * rows, 0)
    return whole


def per_device(activations, cotangent, weights):
    count, channels = activations.shape
    groups, members = lax.axis_size("seq"), lax.axis_size("sub")
    s, j = lax.axis_index("seq"), lax.axis_index("sub")
    place = jnp.stack([s, j]).astype(jnp.int32)
    near, far = DILATION_FIRST // count, DILATION_SECOND // count
    q = count // members
    taps = 3 * channels
    grad_scale = 1.0 / math.sqrt(count * groups * members)

    def kernel(body, *shapes, scratch=(), operands=()):
        return call(body, shapes, scratch, 1, (place,) + tuple(operands))

    def regrouped(block, others=None):
        pieces = [cut(block, j ^ r, q) for r in range(1, members)]
        if others is not None:
            pieces[1:] = after(pieces[1:], others)
        return [swapped(piece, "sub", r + 1) for r, piece in enumerate(pieces)]

    reach = near + far
    act, up_act, down_act = kernel(
        functools.partial(regroup_kernel, (members, q, reach)),
        ((count, channels), BF16),
        ((reach * q, channels), BF16),
        ((reach * q, channels), BF16),
        operands=(activations, *regrouped(activations)),
    )
    low, high = shifted(up_act, "seq", 1), shifted(down_act, "seq", -1)
    w_pieces = gather_pieces(weights, "sub", act)
    c_pieces = regrouped(cotangent, w_pieces[members // 2])

    act_stack, hid_stack, slope_one, slope_two, all_weights = kernel(
        functools.partial(forward_kernel, (groups, members, q, near, far)),
        ((count, taps), BF16),
        ((count, taps), BF16),
        ((count, channels), F32),
        ((count, channels), F32),
        ((2 * taps, channels), BF16),
        scratch=(pltpu.VMEM((members + 2 * far, q, channels), BF16),),
        operands=(low, act, high, *w_pieces),
    )
    delta_two, up_two, down_two, cot = kernel(
        functools.partial(delta_kernel, (members, q, far)),
        ((count, channels), BF16),
        ((far * q, channels), BF16),
        ((far * q, channels), BF16),
        ((count, channels), BF16),
        operands=(slope_two, cotangent, *c_pieces),
    )
    two_low, two_high = shifted(up_two, "seq", 1), shifted(down_two, "seq", -1)
    half = ((taps // 2, channels), F32)
    keep_two, send_two = kernel(
        functools.partial(grad_kernel, (members, 0), grad_scale),
        half,
        half,
        operands=(hid_stack, delta_two),
    )
    shares_two = seq_shares(place, keep_two, swapped(send_two, "sub", 1), ())
    back_one, delta_one = call(
        functools.partial(back_kernel, (members, q, near, far)),
        (((count, channels), F32), ((count, channels), BF16)),
        operands=(two_low, delta_two, two_high, cot, slope_one, all_weights),
    )
    keep_one, send_one, up_one, down_one = kernel(
        functools.partial(grad_kernel, (members, near * q), grad_scale),
        half,
        half,
        ((near * q, channels), BF16),
        ((near * q, channels), BF16),
        operands=(act_stack, delta_one, shares_two[0]),
    )
    one_low, one_high = shifted(up_one, "seq", 1), shifted(down_one, "seq", -1)
    total_two = seq_sum(shares_two)
    shares_one = seq_shares(place, keep_one, swapped(send_one, "sub", 1), (total_two,))
    one_low, one_high = after((one_low, one_high), shares_one)
    part = chip_sum(seq_sum(shares_one), total_two, j)
    sent = part.astype(BF16)

    (grad_in,) = call(
        functools.partial(input_kernel, (members, q, near)),
        (((count, channels), BF16),),
        scalars=1,
        operands=(place, one_low, delta_one, one_high, back_one, all_weights),
    )
    got = [grad_in[r * q : (r + 1) * q] for r in range(members)]
    got = got[:1] + [swapped(got[r], "sub", r) for r in range(1, members)]
    got = after(got, sent)
    input_grad = jnp.zeros((count, channels), BF16)
    for r in range(members):
        input_grad = lax.dynamic_update_slice_in_dim(input_grad, got[r], (j ^ r) * q, 0)

    weight_grad = spread_seq(part, sent, s)
    return (input_grad, weight_grad)


def solution(mesh):
    placed = (P(("grp", "seq", "sub"), None), P(("grp", "seq", "sub"), None), P("sub", None))
    return jax.shard_map(
        per_device,
        mesh=mesh,
        in_specs=placed,
        out_specs=(P(("grp", "seq", "sub"), None), P(("grp", "sub"), None)),
        check_vma=False,
    )
```

```python
import functools
import math

import jax
import jax.numpy as jnp
from jax import lax
from jax.experimental import pallas as pl
from jax.experimental.pallas import tpu as pltpu
from jax.sharding import PartitionSpec as P

DILATION_FIRST = 1024
DILATION_SECOND = 2048
F32 = jnp.float32
BF16 = jnp.bfloat16
SMEM = pl.BlockSpec(memory_space=pltpu.SMEM)
VMEM = pl.BlockSpec(memory_space=pltpu.VMEM)


def shifted(block, axis, distance):
    n = lax.axis_size(axis)
    route = [(i, i + distance) for i in range(n) if 0 <= i + distance < n]
    return lax.ppermute(block, axis, route)


def turned(block, axis, turn):
    n = lax.axis_size(axis)
    return lax.ppermute(block, axis, [(i, (i + turn) % n) for i in range(n)])


def swapped(block, axis, bits):
    n = lax.axis_size(axis)
    return lax.ppermute(block, axis, [(i, i ^ bits) for i in range(n)])


def after(value, others):
    return lax.optimization_barrier((value, others))[0]


def share_of(s, n):
    index, bit = 0, 1
    while bit < n:
        index = 2 * index + lax.rem(s // bit, 2)
        bit *= 2
    return index


def cut(block, index, rows):
    return lax.dynamic_slice_in_dim(block, index * rows, rows, 0)


def gather_pieces(block, axis, others):
    n = lax.axis_size(axis)
    held = {0: block}
    bit = n // 2
    while bit:
        for r in list(held):
            first_far = r == 0 and bit == n // 2
            source = after(held[r], others) if first_far else held[r]
            held[r ^ bit] = swapped(source, axis, bit)
        bit //= 2
    return [held[r] for r in range(n)]


def gelu_parts(v):
    coeff = 0.7978845608
    square = v * v
    return jnp.tanh(v * (coeff + (coeff * 0.044715) * square)), square


def slope_of(v, th, square):
    coeff = 0.7978845608
    inner = 0.5 * coeff + (0.5 * coeff * 3.0 * 0.044715) * square
    return (0.5 + 0.5 * th) + (v * inner) * (1.0 - th * th)


def dot(a, b):
    return jnp.dot(a, b, preferred_element_type=F32)


def back_dot(blocks, w, first):
    channels = w.shape[1]
    total = None
    for k, block in enumerate(blocks):
        tap = w[first + k * channels : first + (k + 1) * channels]
        part = lax.dot_general(block, tap, (((1,), (1,)), ((), ())), preferred_element_type=F32)
        total = part if total is None else total + part
    return total


def regroup_kernel(sizes, place, block, *refs):
    members, q, reach = sizes
    pieces, (own, to_high, to_low) = refs[: members - 1], refs[members - 1 :]
    j = place[1]

    def rows(index):
        return pl.ds(pl.multiple_of(index * q, 16), q)

    own[rows(j), :] = block[rows(j), :]
    for r in range(1, members):
        own[rows(j ^ r), :] = pieces[r - 1][...]
    to_high[...] = own[(members - reach) * q :]
    to_low[...] = own[: reach * q]


def forward_kernel(sizes, place, low, own, high, *refs):
    groups, members, q, near, far = sizes
    w_pieces, (act_stack, hid_stack, slope_one, slope_two, w_out, hid) = (
        refs[:members],
        refs[members:],
    )
    s, j = place[0], place[1]
    reach = near + far
    rows = w_pieces[0].shape[0]
    for r in range(members):
        w_out[pl.ds(pl.multiple_of((j ^ r) * rows, 16), rows), :] = w_pieces[r][...]
    taps = w_out.shape[0] // 2

    def block(b):
        if b < 0:
            return low[(b + reach) * q : (b + reach + 1) * q]
        if b >= members:
            return high[(b - members) * q : (b - members + 1) * q]
        return own[b * q : (b + 1) * q]

    for b in range(-far, members + far):
        stack = jnp.concatenate([block(b - near), block(b), block(b + near)], 1)
        pre = dot(stack, w_out[:taps])
        th, square = gelu_parts(pre)
        half = 0.5 * pre
        value = (block(b).astype(F32) + (half + half * th)).astype(BF16)
        if b < 0:
            value = jnp.where(s > 0, value, jnp.zeros_like(value))
        if b >= members:
            value = jnp.where(s < groups - 1, value, jnp.zeros_like(value))
        hid[b + far] = value
        if 0 <= b < members:
            slope_one[b * q : (b + 1) * q] = slope_of(pre, th, square)
            act_stack[b * q : (b + 1) * q] = stack
    for b in range(members):
        stack = jnp.concatenate([hid[b], hid[b + far], hid[b + 2 * far]], 1)
        here = slice(b * q, (b + 1) * q)
        hid_stack[here] = stack
        pre = dot(stack, w_out[taps:])
        slope_two[here] = slope_of(pre, *gelu_parts(pre))


def delta_kernel(sizes, place, slope, cotangent, *refs):
    members, q, far = sizes
    pieces, (delta, to_high, to_low, cot) = refs[: members - 1], refs[members - 1 :]
    j = place[1]

    def rows(index):
        return pl.ds(pl.multiple_of(index * q, 16), q)

    cot[rows(j), :] = cotangent[rows(j), :]
    for r in range(1, members):
        cot[rows(j ^ r), :] = pieces[r - 1][...]
    for b in range(members):
        here = slice(b * q, (b + 1) * q)
        delta[here] = (cot[here].astype(F32) * slope[here]).astype(BF16)
    to_high[...] = delta[(members - far) * q :]
    to_low[...] = delta[: far * q]


def grad_kernel(sizes, scale, place, stack, delta, *refs):
    members, halo, splits = sizes
    outs = refs[-(1 + splits + (2 if halo else 0)) :]
    keep, sends = outs[0], outs[1 : 1 + splits]
    odd = place[1] & 1
    channels = delta.shape[1]
    rows = 3 * channels // (members // 2)
    share = keep.shape[0] // splits
    for k in range(3):
        first = k * channels
        part = scale * lax.dot_general(
            stack[:, first : first + channels],
            delta[...],
            (((0,), (0,)), ((), ())),
            preferred_element_type=F32,
        )
        for owner in range(members // 2):
            start, stop = max(first, owner * rows), min(first + channels, (owner + 1) * rows)
            if start >= stop:
                continue
            at = (owner // 2) * rows + start - owner * rows
            end = at + stop - start
            value = part[start - first : stop - first]

            @pl.when(odd == owner % 2)
            def _():
                keep[at:end] = value

            @pl.when(odd != owner % 2)
            def _():
                for i in range(splits):
                    low, high = max(at, i * share), min(end, (i + 1) * share)
                    if low < high:
                        sends[i][low - i * share : high - i * share] = value[low - at : high - at]

    if halo:
        to_high, to_low = outs[-2:]
        to_high[...] = delta[delta.shape[0] - halo :]
        to_low[...] = delta[:halo]


def share_kernel(n, splits, place, keep, *refs):
    others, outs, total = refs[:splits], refs[-n - 1 : -1], refs[-1]
    rows = outs[0].shape[0]
    part = keep.shape[0] // splits
    for i in range(splits):
        here = slice(i * part, (i + 1) * part)
        total[here] = keep[here] + others[i][...]
    for turn in range(n):
        index = share_of(lax.rem(place[0] + turn, n), n)
        at = pl.ds(pl.multiple_of(index * rows, 16), rows)
        outs[turn][...] = total[at, :].astype(outs[turn].dtype)


def halve_kernel(bit, place, keep, *refs):
    others, (kept, sent, total) = refs[:-3], refs[-3:]
    rows = keep.shape[0] // len(others)
    for i, other in enumerate(others):
        here = slice(i * rows, (i + 1) * rows)
        total[here] = keep[here] + other[...].astype(F32)
    half = kept.shape[0]
    mine = lax.rem(place[0] // bit, 2)
    kept[...] = total[pl.ds(pl.multiple_of(mine * half, 16), half), :]
    sent[...] = total[pl.ds(pl.multiple_of((1 - mine) * half, 16), half), :].astype(BF16)


def back_kernel(sizes, low, own, high, cot, slope, w, back_one, delta):
    members, q, near, far = sizes

    def block(b):
        if b < 0:
            return low[(b + far) * q : (b + far + 1) * q]
        if b >= members:
            return high[(b - members) * q : (b - members + 1) * q]
        return own[b * q : (b + 1) * q]

    for b in range(members):
        here = slice(b * q, (b + 1) * q)
        product = back_dot((block(b + far), block(b), block(b - far)), w, w.shape[0] // 2)
        back = cot[here].astype(F32) + product
        back_one[here] = back
        delta[here] = (back * slope[here]).astype(BF16)


def input_kernel(sizes, place, low, own, high, back_one, w, out):
    members, q, near = sizes
    j = place[1]

    def block(b):
        if b < 0:
            return low[(b + near) * q : (b + near + 1) * q]
        if b >= members:
            return high[(b - members) * q : (b - members + 1) * q]
        return own[b * q : (b + 1) * q]

    for b in range(members):
        here = slice(b * q, (b + 1) * q)
        product = back_dot((block(b + near), block(b), block(b - near)), w, 0)
        value = (back_one[here] + product).astype(BF16)
        out[pl.ds(pl.multiple_of((j ^ b) * q, 16), q), :] = value


def call(kernel, out_shapes, scratch=(), scalars=0, operands=()):
    specs = [SMEM] * scalars + [VMEM] * (len(operands) - scalars)
    return pl.pallas_call(
        kernel,
        out_shape=tuple(jax.ShapeDtypeStruct(shape, kind) for shape, kind in out_shapes),
        in_specs=specs,
        out_specs=tuple(VMEM for _ in out_shapes),
        scratch_shapes=list(scratch),
        cost_estimate=pl.CostEstimate(flops=1, transcendentals=0, bytes_accessed=1),
        compiler_params=pltpu.CompilerParams(vmem_limit_bytes=8 * 1024 * 1024),
    )(*operands)


def core_sum(place, keep, sends, waits):
    n = lax.axis_size("seq")
    others = [swapped(send, "sub", 1) for send in sends]
    if n > 4:
        return [keep + jnp.concatenate(others, 0)]
    shape = (keep.shape[0] // n, keep.shape[1])
    return call(
        functools.partial(share_kernel, n, len(sends)),
        ((shape, F32),) + ((shape, BF16),) * (n - 1),
        scratch=(pltpu.VMEM(keep.shape, F32),),
        scalars=1,
        operands=(place, keep, *others, *waits),
    )


def seq_parts(shares):
    if len(shares) == 1:
        return [lax.psum(shares[0], "seq")]
    return [shares[0]] + [turned(shares[t], "seq", t) for t in range(1, len(shares))]


def halved(place, keep, others, bit):
    rows, channels = keep.shape
    shape = (rows // 2, channels)
    return call(
        functools.partial(halve_kernel, bit),
        ((shape, F32), (shape, BF16)),
        scratch=(pltpu.VMEM((rows, channels), F32),),
        scalars=1,
        operands=(place, keep, *others),
    )


def core_sum_halving(place, keep, sends):
    others = [swapped(send, "sub", 1) for send in sends]
    n = lax.axis_size("seq")
    if n > 4:
        total = keep + jnp.concatenate(others, 0)
        return total, total
    return halved(place, keep, others, 1)


def first_half(sent):
    return sent if lax.axis_size("seq") > 4 else swapped(sent, "seq", 1)


def seq_sum_halving(place, kept, got, others):
    n = lax.axis_size("seq")
    if n > 4:
        return lax.psum(kept, "seq")
    bit = 2
    while bit < n:
        kept, sent = halved(place, kept, [after(got, others)], bit)
        got = swapped(sent, "seq", bit)
        bit *= 2
    return added([kept, got])


def added(pieces):
    total = pieces[0]
    for piece in pieces[1:]:
        total = total + piece.astype(F32)
    return total


def chip_sum(total_one, total_two, j):
    n = lax.axis_size("sub")
    owned = n // 4
    one = total_one.reshape(owned, -1, total_one.shape[1])
    two = total_two.reshape(owned, -1, total_two.shape[1])
    high = j >= n // 2
    part, send = jnp.where(high, two, one), jnp.where(high, one, two)
    part = part + swapped(send.astype(BF16), "sub", n // 2).astype(F32)
    bit = 2
    while bit < n // 2:
        mine = (j & bit) != 0
        keep, send = jnp.where(mine, part[1::2], part[0::2]), jnp.where(mine, part[0::2], part[1::2])
        part = keep + swapped(send.astype(BF16), "sub", bit).astype(F32)
        bit *= 2
    return part[0]


def spread_seq(total, sent, s):
    n = lax.axis_size("seq")
    if n > 4:
        return total
    rows, channels = total.shape
    whole = jnp.zeros((n * rows, channels), F32)
    whole = lax.dynamic_update_slice_in_dim(whole, total, share_of(s, n) * rows, 0)
    for turn in range(1, n):
        got = turned(sent, "seq", turn).astype(F32)
        at = share_of(lax.rem(s + n - turn, n), n) * rows
        whole = lax.dynamic_update_slice_in_dim(whole, got, at, 0)
    return whole


def per_device(activations, cotangent, weights):
    count, channels = activations.shape
    groups, members = lax.axis_size("seq"), lax.axis_size("sub")
    s, j = lax.axis_index("seq"), lax.axis_index("sub")
    place = jnp.stack([s, j]).astype(jnp.int32)
    near, far = DILATION_FIRST // count, DILATION_SECOND // count
    q = count // members
    taps = 3 * channels
    grad_scale = 1.0 / math.sqrt(count * groups * members)

    def kernel(body, *shapes, scratch=(), operands=()):
        return call(body, shapes, scratch, 1, (place,) + tuple(operands))

    def regrouped(block, others=None):
        pieces = [cut(block, j ^ r, q) for r in range(1, members)]
        if others is not None:
            pieces[1:] = after(pieces[1:], others)
        return [swapped(piece, "sub", r + 1) for r, piece in enumerate(pieces)]

    reach = near + far
    act, up_act, down_act = kernel(
        functools.partial(regroup_kernel, (members, q, reach)),
        ((count, channels), BF16),
        ((reach * q, channels), BF16),
        ((reach * q, channels), BF16),
        operands=(activations, *regrouped(activations)),
    )
    low, high = shifted(up_act, "seq", 1), shifted(down_act, "seq", -1)
    w_pieces = gather_pieces(weights, "sub", act)
    c_pieces = regrouped(cotangent, w_pieces[members // 2])

    act_stack, hid_stack, slope_one, slope_two, all_weights = kernel(
        functools.partial(forward_kernel, (groups, members, q, near, far)),
        ((count, taps), BF16),
        ((count, taps), BF16),
        ((count, channels), F32),
        ((count, channels), F32),
        ((2 * taps, channels), BF16),
        scratch=(pltpu.VMEM((members + 2 * far, q, channels), BF16),),
        operands=(low, act, high, *w_pieces),
    )
    delta_two, up_two, down_two, cot = kernel(
        functools.partial(delta_kernel, (members, q, far)),
        ((count, channels), BF16),
        ((far * q, channels), BF16),
        ((far * q, channels), BF16),
        ((count, channels), BF16),
        operands=(slope_two, cotangent, *c_pieces),
    )
    two_low, two_high = shifted(up_two, "seq", 1), shifted(down_two, "seq", -1)
    splits, more = 8, 8
    half = ((taps // 2, channels), F32)
    share = ((taps // 2 // splits, channels), F32)
    less = ((taps // 2 // more, channels), F32)
    keep_two, *send_two = kernel(
        functools.partial(grad_kernel, (members, 0, splits), grad_scale),
        half,
        *[share] * splits,
        operands=(hid_stack, delta_two),
    )
    kept_two, sent_two = core_sum_halving(place, keep_two, send_two)
    back_one, delta_one = call(
        functools.partial(back_kernel, (members, q, near, far)),
        (((count, channels), F32), ((count, channels), BF16)),
        operands=(two_low, delta_two, two_high, cot, slope_one, all_weights),
    )
    keep_one, *send_one, up_one, down_one = kernel(
        functools.partial(grad_kernel, (members, near * q, more), grad_scale),
        half,
        *[less] * more,
        ((near * q, channels), BF16),
        ((near * q, channels), BF16),
        operands=(act_stack, delta_one),
    )
    got_two = first_half(after(sent_two, (two_low, two_high)))
    shares_one = core_sum(place, keep_one, send_one, (got_two,))
    one_low, one_high = shifted(up_one, "seq", 1), shifted(down_one, "seq", -1)
    parts_one = seq_parts(shares_one)
    total_two = seq_sum_halving(place, kept_two, got_two, shares_one[0])
    total_one = added(parts_one)
    part = chip_sum(total_one, total_two, j)
    sent = part.astype(BF16)

    (grad_in,) = call(
        functools.partial(input_kernel, (members, q, near)),
        (((count, channels), BF16),),
        scalars=1,
        operands=(place, one_low, delta_one, one_high, back_one, all_weights),
    )
    got = [grad_in[r * q : (r + 1) * q] for r in range(members)]
    got = got[:1] + [swapped(got[r], "sub", r) for r in range(1, members)]
    got = after(got, sent)
    input_grad = jnp.zeros((count, channels), BF16)
    for r in range(members):
        input_grad = lax.dynamic_update_slice_in_dim(input_grad, got[r], (j ^ r) * q, 0)

    weight_grad = spread_seq(part, sent, s)
    return (input_grad, weight_grad)


def solution(mesh):
    placed = (P(("grp", "seq", "sub"), None), P(("grp", "seq", "sub"), None), P("sub", None))
    return jax.shard_map(
        per_device,
        mesh=mesh,
        in_specs=placed,
        out_specs=(P(("grp", "seq", "sub"), None), P(("grp", "sub"), None)),
        check_vma=False,
    )
```

```python
import functools
import math

import jax
import jax.numpy as jnp
from jax import lax
from jax.experimental import pallas as pl
from jax.experimental.pallas import tpu as pltpu
from jax.sharding import PartitionSpec as P

DILATION_FIRST = 1024
DILATION_SECOND = 2048
F32 = jnp.float32
BF16 = jnp.bfloat16
SMEM = pl.BlockSpec(memory_space=pltpu.SMEM)
VMEM = pl.BlockSpec(memory_space=pltpu.VMEM)


def shifted(block, axis, distance):
    n = lax.axis_size(axis)
    route = [(i, i + distance) for i in range(n) if 0 <= i + distance < n]
    return lax.ppermute(block, axis, route)


def turned(block, axis, turn):
    n = lax.axis_size(axis)
    return lax.ppermute(block, axis, [(i, (i + turn) % n) for i in range(n)])


def swapped(block, axis, bits):
    n = lax.axis_size(axis)
    return lax.ppermute(block, axis, [(i, i ^ bits) for i in range(n)])


def after(value, others):
    return lax.optimization_barrier((value, others))[0]


def share_of(s, n):
    index, bit = 0, 1
    while bit < n:
        index = 2 * index + lax.rem(s // bit, 2)
        bit *= 2
    return index


def cut(block, index, rows):
    return lax.dynamic_slice_in_dim(block, index * rows, rows, 0)


def gather_pieces(block, axis, others):
    n = lax.axis_size(axis)
    held = {0: block}
    bit = n // 2
    while bit:
        for r in list(held):
            first_far = r == 0 and bit == n // 2
            source = after(held[r], others) if first_far else held[r]
            held[r ^ bit] = swapped(source, axis, bit)
        bit //= 2
    return [held[r] for r in range(n)]


def gelu_parts(v):
    coeff = 0.7978845608
    square = v * v
    return jnp.tanh(v * (coeff + (coeff * 0.044715) * square)), square


def slope_of(v, th, square):
    coeff = 0.7978845608
    inner = 0.5 * coeff + (0.5 * coeff * 3.0 * 0.044715) * square
    return (0.5 + 0.5 * th) + (v * inner) * (1.0 - th * th)


def dot(a, b):
    return jnp.dot(a, b, preferred_element_type=F32)


def back_dot(blocks, w, first):
    channels = w.shape[1]
    total = None
    for k, block in enumerate(blocks):
        tap = w[first + k * channels : first + (k + 1) * channels]
        part = lax.dot_general(block, tap, (((1,), (1,)), ((), ())), preferred_element_type=F32)
        total = part if total is None else total + part
    return total


def regroup_kernel(sizes, place, block, *refs):
    members, q, reach = sizes
    pieces, (own, to_high, to_low) = refs[: members - 1], refs[members - 1 :]
    j = place[1]

    def rows(index):
        return pl.ds(pl.multiple_of(index * q, 16), q)

    own[rows(j), :] = block[rows(j), :]
    for r in range(1, members):
        own[rows(j ^ r), :] = pieces[r - 1][...]
    to_high[...] = own[(members - reach) * q :]
    to_low[...] = own[: reach * q]


def forward_kernel(sizes, place, low, own, high, *refs):
    groups, members, q, near, far = sizes
    w_pieces, (act_stack, hid_stack, slope_one, slope_two, w_out, hid) = (
        refs[:members],
        refs[members:],
    )
    s, j = place[0], place[1]
    reach = near + far
    rows = w_pieces[0].shape[0]
    for r in range(members):
        w_out[pl.ds(pl.multiple_of((j ^ r) * rows, 16), rows), :] = w_pieces[r][...]
    taps = w_out.shape[0] // 2

    def block(b):
        if b < 0:
            return low[(b + reach) * q : (b + reach + 1) * q]
        if b >= members:
            return high[(b - members) * q : (b - members + 1) * q]
        return own[b * q : (b + 1) * q]

    wide = 2 if far % 2 == 0 and members % 2 == 0 else 1

    def first_layer(k):
        stacks = []
        for b in range(k - far, k - far + wide):
            stacks.append(jnp.concatenate([block(b - near), block(b), block(b + near)], 1))
            if 0 <= b < members:
                act_stack[b * q : (b + 1) * q] = stacks[-1]
        return dot(jnp.concatenate(stacks, 0), w_out[:taps])

    def first_end(k, pres):
        for b in range(k - far, k - far + wide):
            pre = pres[(b + far - k) * q : (b + far - k + 1) * q]
            th, square = gelu_parts(pre)
            half = 0.5 * pre
            value = (block(b).astype(F32) + (half + half * th)).astype(BF16)
            if b < 0:
                value = jnp.where(s > 0, value, jnp.zeros_like(value))
            if b >= members:
                value = jnp.where(s < groups - 1, value, jnp.zeros_like(value))
            hid[(b + far) * q : (b + far + 1) * q] = value
            if 0 <= b < members:
                slope_one[b * q : (b + 1) * q] = slope_of(pre, th, square)

    def second_layer(b):
        taken = [hid[(b + k * far) * q : (b + k * far + wide) * q] for k in range(3)]
        stack = jnp.concatenate(taken, 1)
        hid_stack[b * q : (b + wide) * q] = stack
        return dot(stack, w_out[taps:])

    def second_end(b, pre):
        slope_two[b * q : (b + wide) * q] = slope_of(pre, *gelu_parts(pre))

    order, begun = [], 0
    for k in range(0, members + 2 * far, wide):
        order.append((first_layer, first_end, k))
        if k > 2 * far:
            order.append((second_layer, second_end, begun))
            begun += wide
    order += [(second_layer, second_end, b) for b in range(begun, members, wide)]
    last = None
    for product, end, index in order + [(None, None, None)]:
        value = product(index) if product else None
        if last:
            last[0](last[1], last[2])
        last = (end, index, value)


def delta_kernel(sizes, place, slope, cotangent, *refs):
    members, q, far = sizes
    pieces, (delta, to_high, to_low, cot) = refs[: members - 1], refs[members - 1 :]
    j = place[1]

    def rows(index):
        return pl.ds(pl.multiple_of(index * q, 16), q)

    cot[rows(j), :] = cotangent[rows(j), :]
    for r in range(1, members):
        cot[rows(j ^ r), :] = pieces[r - 1][...]
    for b in range(members):
        here = slice(b * q, (b + 1) * q)
        delta[here] = (cot[here].astype(F32) * slope[here]).astype(BF16)
    to_high[...] = delta[(members - far) * q :]
    to_low[...] = delta[: far * q]


def grad_kernel(sizes, scale, place, stack, delta, *refs):
    members, halo, splits = sizes
    outs = refs[-(1 + splits + (2 if halo else 0)) :]
    keep, sends = outs[0], outs[1 : 1 + splits]
    odd = place[1] & 1
    channels = delta.shape[1]
    rows = 3 * channels // (members // 2)
    share = keep.shape[0] // splits
    for k in range(3):
        first = k * channels
        part = scale * lax.dot_general(
            stack[:, first : first + channels],
            delta[...],
            (((0,), (0,)), ((), ())),
            preferred_element_type=F32,
        )
        for owner in range(members // 2):
            start, stop = max(first, owner * rows), min(first + channels, (owner + 1) * rows)
            if start >= stop:
                continue
            at = (owner // 2) * rows + start - owner * rows
            end = at + stop - start
            value = part[start - first : stop - first]

            @pl.when(odd == owner % 2)
            def _():
                keep[at:end] = value

            @pl.when(odd != owner % 2)
            def _():
                for i in range(splits):
                    low, high = max(at, i * share), min(end, (i + 1) * share)
                    if low < high:
                        sends[i][low - i * share : high - i * share] = value[low - at : high - at]

    if halo:
        to_high, to_low = outs[-2:]
        to_high[...] = delta[delta.shape[0] - halo :]
        to_low[...] = delta[:halo]


def share_kernel(n, splits, place, keep, *refs):
    others, outs, total = refs[:splits], refs[-n - 1 : -1], refs[-1]
    rows = outs[0].shape[0]
    part = keep.shape[0] // splits
    for i in range(splits):
        here = slice(i * part, (i + 1) * part)
        total[here] = keep[here] + others[i][...]
    for turn in range(n):
        index = share_of(lax.rem(place[0] + turn, n), n)
        at = pl.ds(pl.multiple_of(index * rows, 16), rows)
        outs[turn][...] = total[at, :].astype(outs[turn].dtype)


def halve_kernel(bit, count, place, keep, *refs):
    others, (kept, sent, total) = refs[:count], refs[-3:]
    rows = keep.shape[0] // len(others)
    for i, other in enumerate(others):
        here = slice(i * rows, (i + 1) * rows)
        total[here] = keep[here] + other[...].astype(F32)
    half = kept.shape[0]
    mine = lax.rem(place[0] // bit, 2)
    kept[...] = total[pl.ds(pl.multiple_of(mine * half, 16), half), :]
    sent[...] = total[pl.ds(pl.multiple_of((1 - mine) * half, 16), half), :].astype(BF16)


def back_kernel(sizes, low, own, high, cot, slope, w, back_one, delta):
    members, q, near, far = sizes

    def block(b):
        if b < 0:
            return low[(b + far) * q : (b + far + 1) * q]
        if b >= members:
            return high[(b - members) * q : (b - members + 1) * q]
        return own[b * q : (b + 1) * q]

    for b in range(members):
        here = slice(b * q, (b + 1) * q)
        product = back_dot((block(b + far), block(b), block(b - far)), w, w.shape[0] // 2)
        back = cot[here].astype(F32) + product
        back_one[here] = back
        delta[here] = (back * slope[here]).astype(BF16)


def input_kernel(sizes, place, low, own, high, back_one, w, out):
    members, q, near = sizes
    j = place[1]

    def block(b):
        if b < 0:
            return low[(b + near) * q : (b + near + 1) * q]
        if b >= members:
            return high[(b - members) * q : (b - members + 1) * q]
        return own[b * q : (b + 1) * q]

    for b in range(members):
        here = slice(b * q, (b + 1) * q)
        product = back_dot((block(b + near), block(b), block(b - near)), w, 0)
        value = (back_one[here] + product).astype(BF16)
        out[pl.ds(pl.multiple_of((j ^ b) * q, 16), q), :] = value


def call(kernel, out_shapes, scratch=(), scalars=0, operands=()):
    specs = [SMEM] * scalars + [VMEM] * (len(operands) - scalars)
    return pl.pallas_call(
        kernel,
        out_shape=tuple(jax.ShapeDtypeStruct(shape, kind) for shape, kind in out_shapes),
        in_specs=specs,
        out_specs=tuple(VMEM for _ in out_shapes),
        scratch_shapes=list(scratch),
        cost_estimate=pl.CostEstimate(flops=1, transcendentals=0, bytes_accessed=1),
        compiler_params=pltpu.CompilerParams(vmem_limit_bytes=8 * 1024 * 1024),
    )(*operands)


def core_sum(place, keep, sends, waits):
    n = lax.axis_size("seq")
    others = [swapped(send, "sub", 1) for send in sends]
    if n > 4:
        return [keep + jnp.concatenate(others, 0)]
    shape = (keep.shape[0] // n, keep.shape[1])
    return call(
        functools.partial(share_kernel, n, len(sends)),
        ((shape, F32),) + ((shape, BF16),) * (n - 1),
        scratch=(pltpu.VMEM(keep.shape, F32),),
        scalars=1,
        operands=(place, keep, *others, *waits),
    )


def seq_parts(shares):
    if len(shares) == 1:
        return [lax.psum(shares[0], "seq")]
    return [shares[0]] + [turned(shares[t], "seq", t) for t in range(1, len(shares))]


def halved(place, keep, others, bit, waits=()):
    rows, channels = keep.shape
    shape = (rows // 2, channels)
    return call(
        functools.partial(halve_kernel, bit, len(others)),
        ((shape, F32), (shape, BF16)),
        scratch=(pltpu.VMEM((rows, channels), F32),),
        scalars=1,
        operands=(place, keep, *others, *waits),
    )


def core_sum_halving(place, keep, sends, waits=()):
    others = [swapped(send, "sub", 1) for send in sends]
    n = lax.axis_size("seq")
    if n > 4:
        total = keep + jnp.concatenate(others, 0)
        return total, total
    return halved(place, keep, others, 1, waits)


def first_half(sent):
    return sent if lax.axis_size("seq") > 4 else swapped(sent, "seq", 1)


def seq_sum_halving(place, kept, got, others):
    n = lax.axis_size("seq")
    if n > 4:
        return lax.psum(kept, "seq")
    bit = 2
    while bit < n:
        came = got if others is None else after(got, others)
        kept, sent = halved(place, kept, [came], bit)
        got = swapped(sent, "seq", bit)
        bit *= 2
    return added([kept, got])


def added(pieces):
    total = pieces[0]
    for piece in pieces[1:]:
        total = total + piece.astype(F32)
    return total


def chip_sum(total_one, total_two, j):
    n = lax.axis_size("sub")
    owned = n // 4
    one = total_one.reshape(owned, -1, total_one.shape[1])
    two = total_two.reshape(owned, -1, total_two.shape[1])
    high = j >= n // 2
    part, send = jnp.where(high, two, one), jnp.where(high, one, two)
    part = part + swapped(send.astype(BF16), "sub", n // 2).astype(F32)
    bit = 2
    while bit < n // 2:
        mine = (j & bit) != 0
        keep, send = jnp.where(mine, part[1::2], part[0::2]), jnp.where(mine, part[0::2], part[1::2])
        part = keep + swapped(send.astype(BF16), "sub", bit).astype(F32)
        bit *= 2
    return part[0]


def spread_seq(total, sent, s):
    n = lax.axis_size("seq")
    if n > 4:
        return total
    rows, channels = total.shape
    whole = jnp.zeros((n * rows, channels), F32)
    whole = lax.dynamic_update_slice_in_dim(whole, total, share_of(s, n) * rows, 0)
    for turn in range(1, n):
        got = turned(sent, "seq", turn).astype(F32)
        at = share_of(lax.rem(s + n - turn, n), n) * rows
        whole = lax.dynamic_update_slice_in_dim(whole, got, at, 0)
    return whole


def per_device(activations, cotangent, weights):
    count, channels = activations.shape
    groups, members = lax.axis_size("seq"), lax.axis_size("sub")
    s, j = lax.axis_index("seq"), lax.axis_index("sub")
    place = jnp.stack([s, j]).astype(jnp.int32)
    near, far = DILATION_FIRST // count, DILATION_SECOND // count
    q = count // members
    taps = 3 * channels
    grad_scale = 1.0 / math.sqrt(count * groups * members)

    def kernel(body, *shapes, scratch=(), operands=()):
        return call(body, shapes, scratch, 1, (place,) + tuple(operands))

    def regrouped(block, others=None):
        pieces = [cut(block, j ^ r, q) for r in range(1, members)]
        if others is not None:
            pieces[1:] = after(pieces[1:], others)
        return [swapped(piece, "sub", r + 1) for r, piece in enumerate(pieces)]

    reach = near + far
    act, up_act, down_act = kernel(
        functools.partial(regroup_kernel, (members, q, reach)),
        ((count, channels), BF16),
        ((reach * q, channels), BF16),
        ((reach * q, channels), BF16),
        operands=(activations, *regrouped(activations)),
    )
    low, high = shifted(up_act, "seq", 1), shifted(down_act, "seq", -1)
    w_pieces = gather_pieces(weights, "sub", act)
    c_pieces = regrouped(cotangent, w_pieces[members // 2])

    act_stack, hid_stack, slope_one, slope_two, all_weights = kernel(
        functools.partial(forward_kernel, (groups, members, q, near, far)),
        ((count, taps), BF16),
        ((count, taps), BF16),
        ((count, channels), F32),
        ((count, channels), F32),
        ((2 * taps, channels), BF16),
        scratch=(pltpu.VMEM(((members + 2 * far) * q, channels), BF16),),
        operands=(low, act, high, *w_pieces),
    )
    delta_two, up_two, down_two, cot = kernel(
        functools.partial(delta_kernel, (members, q, far)),
        ((count, channels), BF16),
        ((far * q, channels), BF16),
        ((far * q, channels), BF16),
        ((count, channels), BF16),
        operands=(slope_two, cotangent, *c_pieces),
    )
    two_low, two_high = shifted(up_two, "seq", 1), shifted(down_two, "seq", -1)
    splits, more = 8, 4
    half = ((taps // 2, channels), F32)
    share = ((taps // 2 // splits, channels), F32)
    less = ((taps // 2 // more, channels), F32)
    keep_two, *send_two = kernel(
        functools.partial(grad_kernel, (members, 0, splits), grad_scale),
        half,
        *[share] * splits,
        operands=(hid_stack, delta_two),
    )
    kept_two, sent_two = core_sum_halving(place, keep_two, send_two)
    back_one, delta_one = call(
        functools.partial(back_kernel, (members, q, near, far)),
        (((count, channels), F32), ((count, channels), BF16)),
        operands=(two_low, delta_two, two_high, cot, slope_one, all_weights),
    )
    keep_one, *send_one, up_one, down_one = kernel(
        functools.partial(grad_kernel, (members, near * q, more), grad_scale),
        half,
        *[less] * more,
        ((near * q, channels), BF16),
        ((near * q, channels), BF16),
        operands=(act_stack, delta_one),
    )
    got_two = first_half(after(sent_two, (two_low, two_high)))
    kept_one, sent_one = core_sum_halving(place, keep_one, send_one, (got_two,))
    got_one = first_half(sent_one)
    up_one, down_one = after((up_one, down_one), sent_one)
    one_low, one_high = shifted(up_one, "seq", 1), shifted(down_one, "seq", -1)
    total_two = seq_sum_halving(place, kept_two, got_two, sent_one)
    total_one = seq_sum_halving(place, kept_one, got_one, None)

    (grad_in,) = call(
        functools.partial(input_kernel, (members, q, near)),
        (((count, channels), BF16),),
        scalars=1,
        operands=(place, one_low, delta_one, one_high, back_one, all_weights),
    )
    total_one = after(total_one, grad_in)
    part = chip_sum(total_one, total_two, j)
    sent = part.astype(BF16)
    got = [grad_in[r * q : (r + 1) * q] for r in range(members)]
    got = got[:1] + [swapped(got[r], "sub", r) for r in range(1, members)]
    got = after(got, sent)
    input_grad = jnp.zeros((count, channels), BF16)
    for r in range(members):
        input_grad = lax.dynamic_update_slice_in_dim(input_grad, got[r], (j ^ r) * q, 0)

    weight_grad = spread_seq(part, sent, s)
    return (input_grad, weight_grad)


def solution(mesh):
    placed = (P(("grp", "seq", "sub"), None), P(("grp", "seq", "sub"), None), P("sub", None))
    return jax.shard_map(
        per_device,
        mesh=mesh,
        in_specs=placed,
        out_specs=(P(("grp", "seq", "sub"), None), P(("grp", "sub"), None)),
        check_vma=False,
    )
```

```python
import functools
import math

import jax
import jax.numpy as jnp
from jax import lax
from jax.experimental import pallas as pl
from jax.experimental.pallas import tpu as pltpu
from jax.sharding import PartitionSpec as P

DILATION_FIRST = 1024
DILATION_SECOND = 2048
F32 = jnp.float32
BF16 = jnp.bfloat16
SMEM = pl.BlockSpec(memory_space=pltpu.SMEM)
VMEM = pl.BlockSpec(memory_space=pltpu.VMEM)


def shifted(block, axis, distance):
    n = lax.axis_size(axis)
    route = [(i, i + distance) for i in range(n) if 0 <= i + distance < n]
    return lax.ppermute(block, axis, route)


def turned(block, axis, turn):
    n = lax.axis_size(axis)
    return lax.ppermute(block, axis, [(i, (i + turn) % n) for i in range(n)])


def swapped(block, axis, bits):
    n = lax.axis_size(axis)
    return lax.ppermute(block, axis, [(i, i ^ bits) for i in range(n)])


def after(value, others):
    return lax.optimization_barrier((value, others))[0]


def share_of(s, n):
    index, bit = 0, 1
    while bit < n:
        index = 2 * index + lax.rem(s // bit, 2)
        bit *= 2
    return index


def cut(block, index, rows):
    return lax.dynamic_slice_in_dim(block, index * rows, rows, 0)


def gather_pieces(block, near, axis, others):
    n = lax.axis_size(axis)
    held = {0: block}
    bit = n // 2
    while bit:
        for r in list(held):
            first_far = r == 0 and bit == n // 2
            source = after(held[r], others) if first_far else held[r]
            held[r ^ bit] = near if r ^ bit == 1 else swapped(source, axis, bit)
        bit //= 2
    return [held[r] for r in range(n)]


def gelu_parts(v):
    coeff = 0.7978845608
    square = v * v
    return jnp.tanh(v * (coeff + (coeff * 0.044715) * square)), square


def slope_of(v, th, square):
    coeff = 0.7978845608
    inner = 0.5 * coeff + (0.5 * coeff * 3.0 * 0.044715) * square
    return (0.5 + 0.5 * th) + (v * inner) * (1.0 - th * th)


def dot(a, b):
    return jnp.dot(a, b, preferred_element_type=F32)


def back_dot(blocks, w, first):
    channels = w.shape[1]
    total = None
    for k, block in enumerate(blocks):
        tap = w[first + k * channels : first + (k + 1) * channels]
        part = lax.dot_general(block, tap, (((1,), (1,)), ((), ())), preferred_element_type=F32)
        total = part if total is None else total + part
    return total


def regroup_kernel(sizes, place, block, *refs):
    members, q, reach = sizes
    pieces, (own, to_high, to_low) = refs[: members - 1], refs[-3:]
    j = place[1]

    def rows(index):
        return pl.ds(pl.multiple_of(index * q, 16), q)

    own[rows(j), :] = block[rows(j), :]
    for r in range(1, members):
        own[rows(j ^ r), :] = pieces[r - 1][...]
    to_high[...] = own[(members - reach) * q :]
    to_low[...] = own[: reach * q]


def forward_kernel(sizes, place, low, own, high, *refs):
    groups, members, q, near, far = sizes
    w_pieces, (act_stack, hid_stack, slope_one, slope_two, w_out, hid) = (
        refs[:members],
        refs[members:],
    )
    s, j = place[0], place[1]
    reach = near + far
    rows = w_pieces[0].shape[0]
    for r in range(members):
        w_out[pl.ds(pl.multiple_of((j ^ r) * rows, 16), rows), :] = w_pieces[r][...]
    taps = w_out.shape[0] // 2

    def block(b):
        if b < 0:
            return low[(b + reach) * q : (b + reach + 1) * q]
        if b >= members:
            return high[(b - members) * q : (b - members + 1) * q]
        return own[b * q : (b + 1) * q]

    wide = 2 if far % 2 == 0 and members % 2 == 0 else 1

    def first_layer(k):
        stacks = []
        for b in range(k - far, k - far + wide):
            stacks.append(jnp.concatenate([block(b - near), block(b), block(b + near)], 1))
            if 0 <= b < members:
                act_stack[b * q : (b + 1) * q] = stacks[-1]
        return dot(jnp.concatenate(stacks, 0), w_out[:taps])

    def first_end(k, pres):
        for b in range(k - far, k - far + wide):
            pre = pres[(b + far - k) * q : (b + far - k + 1) * q]
            th, square = gelu_parts(pre)
            half = 0.5 * pre
            value = (block(b).astype(F32) + (half + half * th)).astype(BF16)
            if b < 0:
                value = jnp.where(s > 0, value, jnp.zeros_like(value))
            if b >= members:
                value = jnp.where(s < groups - 1, value, jnp.zeros_like(value))
            hid[(b + far) * q : (b + far + 1) * q] = value
            if 0 <= b < members:
                slope_one[b * q : (b + 1) * q] = slope_of(pre, th, square)

    def second_layer(b):
        taken = [hid[(b + k * far) * q : (b + k * far + wide) * q] for k in range(3)]
        stack = jnp.concatenate(taken, 1)
        hid_stack[b * q : (b + wide) * q] = stack
        return dot(stack, w_out[taps:])

    def second_end(b, pre):
        slope_two[b * q : (b + wide) * q] = slope_of(pre, *gelu_parts(pre))

    order, begun = [], 0
    for k in range(0, members + 2 * far, wide):
        order.append((first_layer, first_end, k))
        if k > 2 * far:
            order.append((second_layer, second_end, begun))
            begun += wide
    order += [(second_layer, second_end, b) for b in range(begun, members, wide)]
    last = None
    for product, end, index in order + [(None, None, None)]:
        value = product(index) if product else None
        if last:
            last[0](last[1], last[2])
        last = (end, index, value)


def delta_kernel(sizes, place, slope, cotangent, *refs):
    members, q, far = sizes
    pieces, (delta, to_high, to_low, cot) = refs[: members - 1], refs[members - 1 :]
    j = place[1]

    def rows(index):
        return pl.ds(pl.multiple_of(index * q, 16), q)

    cot[rows(j), :] = cotangent[rows(j), :]
    for r in range(1, members):
        cot[rows(j ^ r), :] = pieces[r - 1][...]
    for b in range(members):
        here = slice(b * q, (b + 1) * q)
        delta[here] = (cot[here].astype(F32) * slope[here]).astype(BF16)
    to_high[...] = delta[(members - far) * q :]
    to_low[...] = delta[: far * q]


def grad_kernel(sizes, scale, place, stack, delta, *refs):
    members, halo, splits = sizes
    outs = refs[-(1 + splits + (2 if halo else 0)) :]
    keep, sends = outs[0], outs[1 : 1 + splits]
    odd = place[1] & 1
    channels = delta.shape[1]
    rows = 3 * channels // (members // 2)
    share = keep.shape[0] // splits
    for k in range(3):
        first = k * channels
        part = scale * lax.dot_general(
            stack[:, first : first + channels],
            delta[...],
            (((0,), (0,)), ((), ())),
            preferred_element_type=F32,
        )
        for owner in range(members // 2):
            start, stop = max(first, owner * rows), min(first + channels, (owner + 1) * rows)
            if start >= stop:
                continue
            at = (owner // 2) * rows + start - owner * rows
            end = at + stop - start
            value = part[start - first : stop - first]

            @pl.when(odd == owner % 2)
            def _():
                keep[at:end] = value

            @pl.when(odd != owner % 2)
            def _():
                for i in range(splits):
                    low, high = max(at, i * share), min(end, (i + 1) * share)
                    if low < high:
                        sends[i][low - i * share : high - i * share] = value[low - at : high - at]

    if halo:
        to_high, to_low = outs[-2:]
        to_high[...] = delta[delta.shape[0] - halo :]
        to_low[...] = delta[:halo]


def share_kernel(n, splits, place, keep, *refs):
    others, outs, total = refs[:splits], refs[-n - 1 : -1], refs[-1]
    rows = outs[0].shape[0]
    part = keep.shape[0] // splits
    for i in range(splits):
        here = slice(i * part, (i + 1) * part)
        total[here] = keep[here] + others[i][...]
    for turn in range(n):
        index = share_of(lax.rem(place[0] + turn, n), n)
        at = pl.ds(pl.multiple_of(index * rows, 16), rows)
        outs[turn][...] = total[at, :].astype(outs[turn].dtype)


def halve_kernel(bit, count, place, keep, *refs):
    others, (kept, sent, total) = refs[:count], refs[-3:]
    rows = keep.shape[0] // len(others)
    for i, other in enumerate(others):
        here = slice(i * rows, (i + 1) * rows)
        total[here] = keep[here] + other[...].astype(F32)
    half = kept.shape[0]
    mine = lax.rem(place[0] // bit, 2)
    kept[...] = total[pl.ds(pl.multiple_of(mine * half, 16), half), :]
    sent[...] = total[pl.ds(pl.multiple_of((1 - mine) * half, 16), half), :].astype(BF16)


def back_kernel(sizes, low, own, high, cot, slope, w, back_one, delta):
    members, q, near, far = sizes

    def block(b):
        if b < 0:
            return low[(b + far) * q : (b + far + 1) * q]
        if b >= members:
            return high[(b - members) * q : (b - members + 1) * q]
        return own[b * q : (b + 1) * q]

    for b in range(members):
        here = slice(b * q, (b + 1) * q)
        product = back_dot((block(b + far), block(b), block(b - far)), w, w.shape[0] // 2)
        back = cot[here].astype(F32) + product
        back_one[here] = back
        delta[here] = (back * slope[here]).astype(BF16)


def input_kernel(sizes, place, low, own, high, back_one, w, out):
    members, q, near = sizes
    j = place[1]

    def block(b):
        if b < 0:
            return low[(b + near) * q : (b + near + 1) * q]
        if b >= members:
            return high[(b - members) * q : (b - members + 1) * q]
        return own[b * q : (b + 1) * q]

    for b in range(members):
        here = slice(b * q, (b + 1) * q)
        product = back_dot((block(b + near), block(b), block(b - near)), w, 0)
        value = (back_one[here] + product).astype(BF16)
        out[pl.ds(pl.multiple_of((j ^ b) * q, 16), q), :] = value


def call(kernel, out_shapes, scratch=(), scalars=0, operands=()):
    specs = [SMEM] * scalars + [VMEM] * (len(operands) - scalars)
    return pl.pallas_call(
        kernel,
        out_shape=tuple(jax.ShapeDtypeStruct(shape, kind) for shape, kind in out_shapes),
        in_specs=specs,
        out_specs=tuple(VMEM for _ in out_shapes),
        scratch_shapes=list(scratch),
        cost_estimate=pl.CostEstimate(flops=1, transcendentals=0, bytes_accessed=1),
        compiler_params=pltpu.CompilerParams(vmem_limit_bytes=8 * 1024 * 1024),
    )(*operands)


def core_sum(place, keep, sends, waits):
    n = lax.axis_size("seq")
    others = [swapped(send, "sub", 1) for send in sends]
    if n > 4:
        return [keep + jnp.concatenate(others, 0)]
    shape = (keep.shape[0] // n, keep.shape[1])
    return call(
        functools.partial(share_kernel, n, len(sends)),
        ((shape, F32),) + ((shape, BF16),) * (n - 1),
        scratch=(pltpu.VMEM(keep.shape, F32),),
        scalars=1,
        operands=(place, keep, *others, *waits),
    )


def seq_parts(shares):
    if len(shares) == 1:
        return [lax.psum(shares[0], "seq")]
    return [shares[0]] + [turned(shares[t], "seq", t) for t in range(1, len(shares))]


def halved(place, keep, others, bit, waits=()):
    rows, channels = keep.shape
    shape = (rows // 2, channels)
    return call(
        functools.partial(halve_kernel, bit, len(others)),
        ((shape, F32), (shape, BF16)),
        scratch=(pltpu.VMEM((rows, channels), F32),),
        scalars=1,
        operands=(place, keep, *others, *waits),
    )


def core_sum_halving(place, keep, sends, waits=()):
    others = [swapped(send, "sub", 1) for send in sends]
    n = lax.axis_size("seq")
    if n > 4:
        total = keep + jnp.concatenate(others, 0)
        return total, total
    return halved(place, keep, others, 1, waits)


def first_half(sent):
    return sent if lax.axis_size("seq") > 4 else swapped(sent, "seq", 1)


def seq_sum_halving(place, kept, got, others, waits=()):
    n = lax.axis_size("seq")
    if n > 4:
        return [lax.psum(kept, "seq")]
    bit = 2
    while bit < n:
        came = got if others is None else after(got, others)
        kept, sent = halved(place, kept, [came], bit, waits)
        got = swapped(sent, "seq", bit)
        bit *= 2
    return [kept, got]


def added(pieces):
    total = pieces[0]
    for piece in pieces[1:]:
        total = total + piece.astype(F32)
    return total


def chip_sum(total_one, total_two, j):
    n = lax.axis_size("sub")
    owned = n // 4
    one = total_one.reshape(owned, -1, total_one.shape[1])
    two = total_two.reshape(owned, -1, total_two.shape[1])
    high = j >= n // 2
    part, send = jnp.where(high, two, one), jnp.where(high, one, two)
    part = part + swapped(send.astype(BF16), "sub", n // 2).astype(F32)
    bit = 2
    while bit < n // 2:
        mine = (j & bit) != 0
        keep, send = jnp.where(mine, part[1::2], part[0::2]), jnp.where(mine, part[0::2], part[1::2])
        part = keep + swapped(send.astype(BF16), "sub", bit).astype(F32)
        bit *= 2
    return part[0]


def spread_seq(total, sent, s):
    n = lax.axis_size("seq")
    if n > 4:
        return total
    rows, channels = total.shape
    whole = jnp.zeros((n * rows, channels), F32)
    whole = lax.dynamic_update_slice_in_dim(whole, total, share_of(s, n) * rows, 0)
    for turn in range(1, n):
        got = turned(sent, "seq", turn).astype(F32)
        at = share_of(lax.rem(s + n - turn, n), n) * rows
        whole = lax.dynamic_update_slice_in_dim(whole, got, at, 0)
    return whole


def per_device(activations, cotangent, weights):
    count, channels = activations.shape
    groups, members = lax.axis_size("seq"), lax.axis_size("sub")
    s, j = lax.axis_index("seq"), lax.axis_index("sub")
    place = jnp.stack([s, j]).astype(jnp.int32)
    near, far = DILATION_FIRST // count, DILATION_SECOND // count
    q = count // members
    taps = 3 * channels
    grad_scale = 1.0 / math.sqrt(count * groups * members)

    def kernel(body, *shapes, scratch=(), operands=()):
        return call(body, shapes, scratch, 1, (place,) + tuple(operands))

    def regrouped(block, others=None, first=None):
        pieces = [cut(block, j ^ r, q) for r in range(1, members)]
        if others is not None:
            pieces[1:] = after(pieces[1:], others)
        first = swapped(pieces[0], "sub", 1) if first is None else first
        return [first] + [swapped(piece, "sub", r + 2) for r, piece in enumerate(pieces[1:])]

    reach = near + far
    near_weights = swapped(weights, "sub", 1)
    near_cot = swapped(cut(cotangent, j ^ 1, q), "sub", 1)
    act, up_act, down_act = kernel(
        functools.partial(regroup_kernel, (members, q, reach)),
        ((count, channels), BF16),
        ((reach * q, channels), BF16),
        ((reach * q, channels), BF16),
        operands=(activations, *regrouped(activations), near_weights),
    )
    low, high = shifted(up_act, "seq", 1), shifted(down_act, "seq", -1)
    w_pieces = gather_pieces(weights, near_weights, "sub", act)
    c_pieces = regrouped(cotangent, w_pieces[members // 2], near_cot)

    act_stack, hid_stack, slope_one, slope_two, all_weights = kernel(
        functools.partial(forward_kernel, (groups, members, q, near, far)),
        ((count, taps), BF16),
        ((count, taps), BF16),
        ((count, channels), F32),
        ((count, channels), F32),
        ((2 * taps, channels), BF16),
        scratch=(pltpu.VMEM(((members + 2 * far) * q, channels), BF16),),
        operands=(low, act, high, *w_pieces),
    )
    delta_two, up_two, down_two, cot = kernel(
        functools.partial(delta_kernel, (members, q, far)),
        ((count, channels), BF16),
        ((far * q, channels), BF16),
        ((far * q, channels), BF16),
        ((count, channels), BF16),
        operands=(slope_two, cotangent, *c_pieces),
    )
    two_low, two_high = shifted(up_two, "seq", 1), shifted(down_two, "seq", -1)
    splits, more = 8, 4
    half = ((taps // 2, channels), F32)
    share = ((taps // 2 // splits, channels), F32)
    less = ((taps // 2 // more, channels), F32)
    keep_two, *send_two = kernel(
        functools.partial(grad_kernel, (members, 0, splits), grad_scale),
        half,
        *[share] * splits,
        operands=(hid_stack, delta_two),
    )
    kept_two, sent_two = core_sum_halving(place, keep_two, send_two)
    back_one, delta_one = call(
        functools.partial(back_kernel, (members, q, near, far)),
        (((count, channels), F32), ((count, channels), BF16)),
        operands=(two_low, delta_two, two_high, cot, slope_one, all_weights),
    )
    keep_one, *send_one, up_one, down_one = kernel(
        functools.partial(grad_kernel, (members, near * q, more), grad_scale),
        half,
        *[less] * more,
        ((near * q, channels), BF16),
        ((near * q, channels), BF16),
        operands=(act_stack, delta_one),
    )
    got_two = first_half(after(sent_two, (two_low, two_high)))
    kept_one, sent_one = core_sum_halving(place, keep_one, send_one, (got_two,))
    got_one = first_half(sent_one)
    up_one, down_one = after((up_one, down_one), sent_one)
    one_low, one_high = shifted(up_one, "seq", 1), shifted(down_one, "seq", -1)
    parts_two = seq_sum_halving(place, kept_two, got_two, sent_one)
    parts_one = seq_sum_halving(place, kept_one, got_one, None, parts_two[1:])

    (grad_in,) = call(
        functools.partial(input_kernel, (members, q, near)),
        (((count, channels), BF16),),
        scalars=1,
        operands=(place, one_low, delta_one, one_high, back_one, all_weights),
    )
    total_one = added(after(parts_one, grad_in))
    total_two = added(parts_two)
    part = chip_sum(total_one, total_two, j)
    sent = part.astype(BF16)
    got = [grad_in[r * q : (r + 1) * q] for r in range(members)]
    got = got[:1] + [swapped(got[r], "sub", r) for r in range(1, members)]
    got = after(got, sent)
    input_grad = jnp.zeros((count, channels), BF16)
    for r in range(members):
        input_grad = lax.dynamic_update_slice_in_dim(input_grad, got[r], (j ^ r) * q, 0)

    weight_grad = spread_seq(part, sent, s)
    return (input_grad, weight_grad)


def solution(mesh):
    placed = (P(("grp", "seq", "sub"), None), P(("grp", "seq", "sub"), None), P("sub", None))
    return jax.shard_map(
        per_device,
        mesh=mesh,
        in_specs=placed,
        out_specs=(P(("grp", "seq", "sub"), None), P(("grp", "sub"), None)),
        check_vma=False,
    )
```

```python
import functools
import math

import jax
import jax.numpy as jnp
from jax import lax
from jax.experimental import pallas as pl
from jax.experimental.pallas import tpu as pltpu
from jax.sharding import PartitionSpec as P

DILATION_FIRST = 1024
DILATION_SECOND = 2048
F32 = jnp.float32
BF16 = jnp.bfloat16
SMEM = pl.BlockSpec(memory_space=pltpu.SMEM)
VMEM = pl.BlockSpec(memory_space=pltpu.VMEM)


def shifted(block, axis, distance):
    n = lax.axis_size(axis)
    route = [(i, i + distance) for i in range(n) if 0 <= i + distance < n]
    return lax.ppermute(block, axis, route)


def turned(block, axis, turn):
    n = lax.axis_size(axis)
    return lax.ppermute(block, axis, [(i, (i + turn) % n) for i in range(n)])


def swapped(block, axis, bits):
    n = lax.axis_size(axis)
    return lax.ppermute(block, axis, [(i, i ^ bits) for i in range(n)])


def after(value, others):
    return lax.optimization_barrier((value, others))[0]


def share_of(s, n):
    index, bit = 0, 1
    while bit < n:
        index = 2 * index + lax.rem(s // bit, 2)
        bit *= 2
    return index


def cut(block, index, rows):
    return lax.dynamic_slice_in_dim(block, index * rows, rows, 0)


def gather_pieces(block, near, axis, others):
    n = lax.axis_size(axis)
    held = {0: block}
    bit = n // 2
    while bit:
        for r in list(held):
            first_far = r == 0 and bit == n // 2
            source = after(held[r], others) if first_far else held[r]
            held[r ^ bit] = near if r ^ bit == 1 else swapped(source, axis, bit)
        bit //= 2
    return [held[r] for r in range(n)]


def gelu_parts(v):
    coeff = 0.7978845608
    square = v * v
    return jnp.tanh(v * (coeff + (coeff * 0.044715) * square)), square


def slope_of(v, th, square):
    coeff = 0.7978845608
    inner = 0.5 * coeff + (0.5 * coeff * 3.0 * 0.044715) * square
    return (0.5 + 0.5 * th) + (v * inner) * (1.0 - th * th)


def dot(a, b):
    return jnp.dot(a, b, preferred_element_type=F32)


def back_dot(blocks, w, first):
    channels = w.shape[1]
    total = None
    for k, block in enumerate(blocks):
        tap = w[first + k * channels : first + (k + 1) * channels]
        part = lax.dot_general(block, tap, (((1,), (1,)), ((), ())), preferred_element_type=F32)
        total = part if total is None else total + part
    return total


def regroup_kernel(sizes, place, block, *refs):
    members, q, reach = sizes
    pieces, (own, to_high, to_low) = refs[: members - 1], refs[-3:]
    j = place[1]

    def rows(index):
        return pl.ds(pl.multiple_of(index * q, 16), q)

    own[rows(j), :] = block[rows(j), :]
    for r in range(1, members):
        own[rows(j ^ r), :] = pieces[r - 1][...]
    to_high[...] = own[(members - reach) * q :]
    to_low[...] = own[: reach * q]


def forward_kernel(sizes, place, low, own, high, *refs):
    groups, members, q, near, far = sizes
    w_pieces, (hid, slope_one, slope_two, w_out) = (
        refs[:members],
        refs[members:],
    )
    s, j = place[0], place[1]
    reach = near + far
    rows = w_pieces[0].shape[0]
    for r in range(members):
        w_out[pl.ds(pl.multiple_of((j ^ r) * rows, 16), rows), :] = w_pieces[r][...]
    taps = w_out.shape[0] // 2

    def block(b):
        if b < 0:
            return low[(b + reach) * q : (b + reach + 1) * q]
        if b >= members:
            return high[(b - members) * q : (b - members + 1) * q]
        return own[b * q : (b + 1) * q]

    wide = 2 if far % 2 == 0 and members % 2 == 0 else 1

    def first_layer(k):
        stacks = []
        for b in range(k - far, k - far + wide):
            stacks.append(jnp.concatenate([block(b - near), block(b), block(b + near)], 1))
        return dot(jnp.concatenate(stacks, 0), w_out[:taps])

    def first_end(k, pres):
        for b in range(k - far, k - far + wide):
            pre = pres[(b + far - k) * q : (b + far - k + 1) * q]
            th, square = gelu_parts(pre)
            half = 0.5 * pre
            value = (block(b).astype(F32) + (half + half * th)).astype(BF16)
            if b < 0:
                value = jnp.where(s > 0, value, jnp.zeros_like(value))
            if b >= members:
                value = jnp.where(s < groups - 1, value, jnp.zeros_like(value))
            hid[(b + far) * q : (b + far + 1) * q] = value
            if 0 <= b < members:
                slope_one[b * q : (b + 1) * q] = slope_of(pre, th, square)

    def second_layer(b):
        taken = [hid[(b + k * far) * q : (b + k * far + wide) * q] for k in range(3)]
        stack = jnp.concatenate(taken, 1)
        return dot(stack, w_out[taps:])

    def second_end(b, pre):
        slope_two[b * q : (b + wide) * q] = slope_of(pre, *gelu_parts(pre))

    order, begun = [], 0
    for k in range(0, members + 2 * far, wide):
        order.append((first_layer, first_end, k))
        if k > 2 * far:
            order.append((second_layer, second_end, begun))
            begun += wide
    order += [(second_layer, second_end, b) for b in range(begun, members, wide)]
    last = None
    for product, end, index in order + [(None, None, None)]:
        value = product(index) if product else None
        if last:
            last[0](last[1], last[2])
        last = (end, index, value)


def delta_kernel(sizes, place, slope, cotangent, *refs):
    members, q, far = sizes
    pieces, (delta, to_high, to_low, cot) = refs[: members - 1], refs[members - 1 :]
    j = place[1]

    def rows(index):
        return pl.ds(pl.multiple_of(index * q, 16), q)

    cot[rows(j), :] = cotangent[rows(j), :]
    for r in range(1, members):
        cot[rows(j ^ r), :] = pieces[r - 1][...]
    for b in range(members):
        here = slice(b * q, (b + 1) * q)
        delta[here] = (cot[here].astype(F32) * slope[here]).astype(BF16)
    to_high[...] = delta[(members - far) * q :]
    to_low[...] = delta[: far * q]


def window(low, own, high, shift):
    rows = own.shape[0]
    if shift < 0:
        return jnp.concatenate([low[low.shape[0] + shift :], own[: rows + shift]], 0)
    if shift > 0:
        return jnp.concatenate([own[shift:], high[:shift]], 0)
    return own[...]


def grad_kernel(sizes, scale, place, low, own, high, delta, *refs):
    members, halo, splits, step = sizes
    outs = refs[-(1 + splits + (2 if halo else 0)) :]
    keep, sends = outs[0], outs[1 : 1 + splits]
    odd = place[1] & 1
    channels = delta.shape[1]
    rows = 3 * channels // (members // 2)
    share = keep.shape[0] // splits
    for k in range(3):
        first = k * channels
        part = scale * lax.dot_general(
            window(low, own, high, (k - 1) * step),
            delta[...],
            (((0,), (0,)), ((), ())),
            preferred_element_type=F32,
        )
        for owner in range(members // 2):
            start, stop = max(first, owner * rows), min(first + channels, (owner + 1) * rows)
            if start >= stop:
                continue
            at = (owner // 2) * rows + start - owner * rows
            end = at + stop - start
            value = part[start - first : stop - first]

            @pl.when(odd == owner % 2)
            def _():
                keep[at:end] = value

            @pl.when(odd != owner % 2)
            def _():
                for i in range(splits):
                    low, high = max(at, i * share), min(end, (i + 1) * share)
                    if low < high:
                        sends[i][low - i * share : high - i * share] = value[low - at : high - at]

    if halo:
        to_high, to_low = outs[-2:]
        to_high[...] = delta[delta.shape[0] - halo :]
        to_low[...] = delta[:halo]


def grad_two_kernel(sizes, scale, place, hidden, delta, *refs):
    step, rows = sizes[3], delta.shape[0]
    low, own, high = hidden.at[:step], hidden.at[step : step + rows], hidden.at[step + rows :]
    grad_kernel(sizes, scale, place, low, own, high, delta, *refs)


def share_kernel(n, splits, place, keep, *refs):
    others, outs, total = refs[:splits], refs[-n - 1 : -1], refs[-1]
    rows = outs[0].shape[0]
    part = keep.shape[0] // splits
    for i in range(splits):
        here = slice(i * part, (i + 1) * part)
        total[here] = keep[here] + others[i][...]
    for turn in range(n):
        index = share_of(lax.rem(place[0] + turn, n), n)
        at = pl.ds(pl.multiple_of(index * rows, 16), rows)
        outs[turn][...] = total[at, :].astype(outs[turn].dtype)


def halve_kernel(bit, count, place, keep, *refs):
    others, (kept, sent, total) = refs[:count], refs[-3:]
    rows = keep.shape[0] // len(others)
    for i, other in enumerate(others):
        here = slice(i * rows, (i + 1) * rows)
        total[here] = keep[here] + other[...].astype(F32)
    half = kept.shape[0]
    mine = lax.rem(place[0] // bit, 2)
    kept[...] = total[pl.ds(pl.multiple_of(mine * half, 16), half), :]
    sent[...] = total[pl.ds(pl.multiple_of((1 - mine) * half, 16), half), :].astype(BF16)


def back_kernel(sizes, low, own, high, cot, slope, w, back_one, delta):
    members, q, near, far = sizes

    def block(b):
        if b < 0:
            return low[(b + far) * q : (b + far + 1) * q]
        if b >= members:
            return high[(b - members) * q : (b - members + 1) * q]
        return own[b * q : (b + 1) * q]

    for b in range(members):
        here = slice(b * q, (b + 1) * q)
        product = back_dot((block(b + far), block(b), block(b - far)), w, w.shape[0] // 2)
        back = cot[here].astype(F32) + product
        back_one[here] = back
        delta[here] = (back * slope[here]).astype(BF16)


def input_kernel(sizes, place, low, own, high, back_one, w, out):
    members, q, near = sizes
    j = place[1]

    def block(b):
        if b < 0:
            return low[(b + near) * q : (b + near + 1) * q]
        if b >= members:
            return high[(b - members) * q : (b - members + 1) * q]
        return own[b * q : (b + 1) * q]

    for b in range(members):
        here = slice(b * q, (b + 1) * q)
        product = back_dot((block(b + near), block(b), block(b - near)), w, 0)
        value = (back_one[here] + product).astype(BF16)
        out[pl.ds(pl.multiple_of((j ^ b) * q, 16), q), :] = value


def call(kernel, out_shapes, scratch=(), scalars=0, operands=()):
    specs = [SMEM] * scalars + [VMEM] * (len(operands) - scalars)
    return pl.pallas_call(
        kernel,
        out_shape=tuple(jax.ShapeDtypeStruct(shape, kind) for shape, kind in out_shapes),
        in_specs=specs,
        out_specs=tuple(VMEM for _ in out_shapes),
        scratch_shapes=list(scratch),
        cost_estimate=pl.CostEstimate(flops=1, transcendentals=0, bytes_accessed=1),
        compiler_params=pltpu.CompilerParams(vmem_limit_bytes=8 * 1024 * 1024),
    )(*operands)


def core_sum(place, keep, sends, waits):
    n = lax.axis_size("seq")
    others = [swapped(send, "sub", 1) for send in sends]
    if n > 4:
        return [keep + jnp.concatenate(others, 0)]
    shape = (keep.shape[0] // n, keep.shape[1])
    return call(
        functools.partial(share_kernel, n, len(sends)),
        ((shape, F32),) + ((shape, BF16),) * (n - 1),
        scratch=(pltpu.VMEM(keep.shape, F32),),
        scalars=1,
        operands=(place, keep, *others, *waits),
    )


def seq_parts(shares):
    if len(shares) == 1:
        return [lax.psum(shares[0], "seq")]
    return [shares[0]] + [turned(shares[t], "seq", t) for t in range(1, len(shares))]


def halved(place, keep, others, bit, waits=()):
    rows, channels = keep.shape
    shape = (rows // 2, channels)
    return call(
        functools.partial(halve_kernel, bit, len(others)),
        ((shape, F32), (shape, BF16)),
        scratch=(pltpu.VMEM((rows, channels), F32),),
        scalars=1,
        operands=(place, keep, *others, *waits),
    )


def core_sum_halving(place, keep, sends, waits=()):
    others = [swapped(send, "sub", 1) for send in sends]
    n = lax.axis_size("seq")
    if n > 4:
        total = keep + jnp.concatenate(others, 0)
        return total, total
    return halved(place, keep, others, 1, waits)


def first_half(sent):
    return sent if lax.axis_size("seq") > 4 else swapped(sent, "seq", 1)


def seq_sum_halving(place, kept, got, others, waits=()):
    n = lax.axis_size("seq")
    if n > 4:
        return [lax.psum(kept, "seq")]
    bit = 2
    while bit < n:
        came = got if others is None else after(got, others)
        kept, sent = halved(place, kept, [came], bit, waits)
        got = swapped(sent, "seq", bit)
        bit *= 2
    return [kept, got]


def added(pieces):
    total = pieces[0]
    for piece in pieces[1:]:
        total = total + piece.astype(F32)
    return total


def chip_sum(total_one, total_two, j):
    n = lax.axis_size("sub")
    owned = n // 4
    one = total_one.reshape(owned, -1, total_one.shape[1])
    two = total_two.reshape(owned, -1, total_two.shape[1])
    high = j >= n // 2
    part, send = jnp.where(high, two, one), jnp.where(high, one, two)
    part = part + swapped(send.astype(BF16), "sub", n // 2).astype(F32)
    bit = 2
    while bit < n // 2:
        mine = (j & bit) != 0
        keep, send = jnp.where(mine, part[1::2], part[0::2]), jnp.where(mine, part[0::2], part[1::2])
        part = keep + swapped(send.astype(BF16), "sub", bit).astype(F32)
        bit *= 2
    return part[0]


def spread_seq(total, sent, s):
    n = lax.axis_size("seq")
    if n > 4:
        return total
    rows, channels = total.shape
    whole = jnp.zeros((n * rows, channels), F32)
    whole = lax.dynamic_update_slice_in_dim(whole, total, share_of(s, n) * rows, 0)
    for turn in range(1, n):
        got = turned(sent, "seq", turn).astype(F32)
        at = share_of(lax.rem(s + n - turn, n), n) * rows
        whole = lax.dynamic_update_slice_in_dim(whole, got, at, 0)
    return whole


def per_device(activations, cotangent, weights):
    count, channels = activations.shape
    groups, members = lax.axis_size("seq"), lax.axis_size("sub")
    s, j = lax.axis_index("seq"), lax.axis_index("sub")
    place = jnp.stack([s, j]).astype(jnp.int32)
    near, far = DILATION_FIRST // count, DILATION_SECOND // count
    q = count // members
    taps = 3 * channels
    grad_scale = 1.0 / math.sqrt(count * groups * members)

    def kernel(body, *shapes, scratch=(), operands=()):
        return call(body, shapes, scratch, 1, (place,) + tuple(operands))

    def regrouped(block, others=None, first=None):
        pieces = [cut(block, j ^ r, q) for r in range(1, members)]
        if others is not None:
            pieces[1:] = after(pieces[1:], others)
        first = swapped(pieces[0], "sub", 1) if first is None else first
        return [first] + [swapped(piece, "sub", r + 2) for r, piece in enumerate(pieces[1:])]

    reach = near + far
    near_weights = swapped(weights, "sub", 1)
    near_cot = swapped(cut(cotangent, j ^ 1, q), "sub", 1)
    act, up_act, down_act = kernel(
        functools.partial(regroup_kernel, (members, q, reach)),
        ((count, channels), BF16),
        ((reach * q, channels), BF16),
        ((reach * q, channels), BF16),
        operands=(activations, *regrouped(activations), near_weights),
    )
    low, high = shifted(up_act, "seq", 1), shifted(down_act, "seq", -1)
    w_pieces = gather_pieces(weights, near_weights, "sub", act)
    c_pieces = regrouped(cotangent, w_pieces[members // 2], near_cot)

    hidden, slope_one, slope_two, all_weights = kernel(
        functools.partial(forward_kernel, (groups, members, q, near, far)),
        ((count + 2 * far * q, channels), BF16),
        ((count, channels), F32),
        ((count, channels), F32),
        ((2 * taps, channels), BF16),
        operands=(low, act, high, *w_pieces),
    )
    delta_two, up_two, down_two, cot = kernel(
        functools.partial(delta_kernel, (members, q, far)),
        ((count, channels), BF16),
        ((far * q, channels), BF16),
        ((far * q, channels), BF16),
        ((count, channels), BF16),
        operands=(slope_two, cotangent, *c_pieces),
    )
    two_low, two_high = shifted(up_two, "seq", 1), shifted(down_two, "seq", -1)
    splits, more = 8, 4
    half = ((taps // 2, channels), F32)
    share = ((taps // 2 // splits, channels), F32)
    less = ((taps // 2 // more, channels), F32)
    keep_two, *send_two = kernel(
        functools.partial(grad_two_kernel, (members, 0, splits, far * q), grad_scale),
        half,
        *[share] * splits,
        operands=(hidden, delta_two),
    )
    kept_two, sent_two = core_sum_halving(place, keep_two, send_two)
    back_one, delta_one = call(
        functools.partial(back_kernel, (members, q, near, far)),
        (((count, channels), F32), ((count, channels), BF16)),
        operands=(two_low, delta_two, two_high, cot, slope_one, all_weights),
    )
    keep_one, *send_one, up_one, down_one = kernel(
        functools.partial(grad_kernel, (members, near * q, more, near * q), grad_scale),
        half,
        *[less] * more,
        ((near * q, channels), BF16),
        ((near * q, channels), BF16),
        operands=(low, act, high, delta_one),
    )
    got_two = first_half(after(sent_two, (two_low, two_high)))
    kept_one, sent_one = core_sum_halving(place, keep_one, send_one, (got_two,))
    got_one = first_half(sent_one)
    up_one, down_one = after((up_one, down_one), sent_one)
    one_low, one_high = shifted(up_one, "seq", 1), shifted(down_one, "seq", -1)
    parts_two = seq_sum_halving(place, kept_two, got_two, sent_one)
    parts_one = seq_sum_halving(place, kept_one, got_one, None, parts_two[1:])

    (grad_in,) = call(
        functools.partial(input_kernel, (members, q, near)),
        (((count, channels), BF16),),
        scalars=1,
        operands=(place, one_low, delta_one, one_high, back_one, all_weights),
    )
    total_one = added(after(parts_one, (one_low, one_high)))
    total_two = added(parts_two)
    part = chip_sum(total_one, total_two, j)
    sent = part.astype(BF16)
    got = [grad_in[r * q : (r + 1) * q] for r in range(members)]
    got = got[:1] + [swapped(got[r], "sub", r) for r in range(1, members)]
    got = after(got, sent)
    input_grad = jnp.zeros((count, channels), BF16)
    for r in range(members):
        input_grad = lax.dynamic_update_slice_in_dim(input_grad, got[r], (j ^ r) * q, 0)

    weight_grad = spread_seq(part, sent, s)
    return (input_grad, weight_grad)


def solution(mesh):
    placed = (P(("grp", "seq", "sub"), None), P(("grp", "seq", "sub"), None), P("sub", None))
    return jax.shard_map(
        per_device,
        mesh=mesh,
        in_specs=placed,
        out_specs=(P(("grp", "seq", "sub"), None), P(("grp", "sub"), None)),
        check_vma=False,
    )
```

```python
import functools
import math

import jax
import jax.numpy as jnp
from jax import lax
from jax.experimental import pallas as pl
from jax.experimental.pallas import tpu as pltpu
from jax.sharding import PartitionSpec as P

DILATION_FIRST = 1024
DILATION_SECOND = 2048
F32 = jnp.float32
BF16 = jnp.bfloat16
SMEM = pl.BlockSpec(memory_space=pltpu.SMEM)
VMEM = pl.BlockSpec(memory_space=pltpu.VMEM)


def shifted(block, axis, distance):
    n = lax.axis_size(axis)
    route = [(i, i + distance) for i in range(n) if 0 <= i + distance < n]
    return lax.ppermute(block, axis, route)


def turned(block, axis, turn):
    n = lax.axis_size(axis)
    return lax.ppermute(block, axis, [(i, (i + turn) % n) for i in range(n)])


def swapped(block, axis, bits):
    n = lax.axis_size(axis)
    return lax.ppermute(block, axis, [(i, i ^ bits) for i in range(n)])


def after(value, others):
    return lax.optimization_barrier((value, others))[0]


def share_of(s, n):
    index, bit = 0, 1
    while bit < n:
        index = 2 * index + lax.rem(s // bit, 2)
        bit *= 2
    return index


def cut(block, index, rows):
    return lax.dynamic_slice_in_dim(block, index * rows, rows, 0)


def gather_pieces(block, near, axis, others):
    n = lax.axis_size(axis)
    held = {0: block}
    bit = n // 2
    while bit:
        for r in list(held):
            first_far = r == 0 and bit == n // 2
            source = after(held[r], others) if first_far else held[r]
            held[r ^ bit] = near if r ^ bit == 1 else swapped(source, axis, bit)
        bit //= 2
    return [held[r] for r in range(n)]


def gelu_parts(v):
    coeff = 0.7978845608
    square = v * v
    return jnp.tanh(v * (coeff + (coeff * 0.044715) * square)), square


def slope_of(v, th, square):
    coeff = 0.7978845608
    inner = 0.5 * coeff + (0.5 * coeff * 3.0 * 0.044715) * square
    return (0.5 + 0.5 * th) + (v * inner) * (1.0 - th * th)


def dot(a, b):
    return jnp.dot(a, b, preferred_element_type=F32)


def back_dot(blocks, w, first):
    channels = w.shape[1]
    total = None
    for k, block in enumerate(blocks):
        tap = w[first + k * channels : first + (k + 1) * channels]
        part = lax.dot_general(block, tap, (((1,), (1,)), ((), ())), preferred_element_type=F32)
        total = part if total is None else total + part
    return total


def regroup_kernel(sizes, place, block, *refs):
    members, q, reach = sizes
    pieces, (own, to_high, to_low) = refs[: members - 1], refs[-3:]
    j = place[1]

    def rows(index):
        return pl.ds(pl.multiple_of(index * q, 16), q)

    own[rows(j), :] = block[rows(j), :]
    for r in range(1, members):
        own[rows(j ^ r), :] = pieces[r - 1][...]
    to_high[...] = own[(members - reach) * q :]
    to_low[...] = own[: reach * q]


def forward_kernel(sizes, place, low, own, high, *refs):
    groups, members, q, near, far = sizes
    w_pieces, (hid, slope_one, slope_two, w_out) = (
        refs[:members],
        refs[members:],
    )
    s, j = place[0], place[1]
    reach = near + far
    rows = w_pieces[0].shape[0]
    for r in range(members):
        w_out[pl.ds(pl.multiple_of((j ^ r) * rows, 16), rows), :] = w_pieces[r][...]
    taps = w_out.shape[0] // 2

    def block(b):
        if b < 0:
            return low[(b + reach) * q : (b + reach + 1) * q]
        if b >= members:
            return high[(b - members) * q : (b - members + 1) * q]
        return own[b * q : (b + 1) * q]

    wide = 2 if far % 2 == 0 and members % 2 == 0 else 1

    def first_layer(k):
        stacks = []
        for b in range(k - far, k - far + wide):
            stacks.append(jnp.concatenate([block(b - near), block(b), block(b + near)], 1))
        return dot(jnp.concatenate(stacks, 0), w_out[:taps])

    def first_end(k, pres):
        for b in range(k - far, k - far + wide):
            pre = pres[(b + far - k) * q : (b + far - k + 1) * q]
            th, square = gelu_parts(pre)
            half = 0.5 * pre
            value = (block(b).astype(F32) + (half + half * th)).astype(BF16)
            if b < 0:
                value = jnp.where(s > 0, value, jnp.zeros_like(value))
            if b >= members:
                value = jnp.where(s < groups - 1, value, jnp.zeros_like(value))
            hid[(b + far) * q : (b + far + 1) * q] = value
            if 0 <= b < members:
                slope_one[b * q : (b + 1) * q] = slope_of(pre, th, square)

    def second_layer(b):
        taken = [hid[(b + k * far) * q : (b + k * far + wide) * q] for k in range(3)]
        stack = jnp.concatenate(taken, 1)
        return dot(stack, w_out[taps:])

    def second_end(b, pre):
        slope_two[b * q : (b + wide) * q] = slope_of(pre, *gelu_parts(pre))

    order, begun = [], 0
    for k in range(0, members + 2 * far, wide):
        order.append((first_layer, first_end, k))
        if k > 2 * far:
            order.append((second_layer, second_end, begun))
            begun += wide
    order += [(second_layer, second_end, b) for b in range(begun, members, wide)]
    last = None
    for product, end, index in order + [(None, None, None)]:
        value = product(index) if product else None
        if last:
            last[0](last[1], last[2])
        last = (end, index, value)


def delta_kernel(sizes, place, slope, cotangent, *refs):
    members, q, far = sizes
    pieces, (delta, to_high, to_low, cot) = refs[: members - 1], refs[members - 1 :]
    j = place[1]

    def rows(index):
        return pl.ds(pl.multiple_of(index * q, 16), q)

    cot[rows(j), :] = cotangent[rows(j), :]
    for r in range(1, members):
        cot[rows(j ^ r), :] = pieces[r - 1][...]
    for b in range(members):
        here = slice(b * q, (b + 1) * q)
        delta[here] = (cot[here].astype(F32) * slope[here]).astype(BF16)
    to_high[...] = delta[(members - far) * q :]
    to_low[...] = delta[: far * q]


def window(low, own, high, shift):
    rows = own.shape[0]
    if shift < 0:
        return jnp.concatenate([low[low.shape[0] + shift :], own[: rows + shift]], 0)
    if shift > 0:
        return jnp.concatenate([own[shift:], high[:shift]], 0)
    return own[...]


def grad_kernel(sizes, scale, place, low, own, high, delta, *refs):
    members, halo, splits, step = sizes
    outs = refs[-(1 + splits + (2 if halo else 0)) :]
    keep, sends = outs[0], outs[1 : 1 + splits]
    odd = place[1] & 1
    channels = delta.shape[1]
    rows = 3 * channels // (members // 2)
    share = keep.shape[0] // splits
    for k in range(3):
        first = k * channels
        part = scale * lax.dot_general(
            window(low, own, high, (k - 1) * step),
            delta[...],
            (((0,), (0,)), ((), ())),
            preferred_element_type=F32,
        )
        for owner in range(members // 2):
            start, stop = max(first, owner * rows), min(first + channels, (owner + 1) * rows)
            if start >= stop:
                continue
            at = (owner // 2) * rows + start - owner * rows
            end = at + stop - start
            value = part[start - first : stop - first]

            @pl.when(odd == owner % 2)
            def _():
                keep[at:end] = value

            @pl.when(odd != owner % 2)
            def _():
                for i in range(splits):
                    low, high = max(at, i * share), min(end, (i + 1) * share)
                    if low < high:
                        piece = value[low - at : high - at].astype(sends[i].dtype)
                        sends[i][low - i * share : high - i * share] = piece

    if halo:
        to_high, to_low = outs[-2:]
        to_high[...] = delta[delta.shape[0] - halo :]
        to_low[...] = delta[:halo]


def grad_two_kernel(sizes, scale, place, hidden, delta, *refs):
    step, rows = sizes[3], delta.shape[0]
    low, own, high = hidden.at[:step], hidden.at[step : step + rows], hidden.at[step + rows :]
    grad_kernel(sizes, scale, place, low, own, high, delta, *refs)


def share_kernel(n, splits, place, keep, *refs):
    others, outs, total = refs[:splits], refs[-n - 1 : -1], refs[-1]
    rows = outs[0].shape[0]
    part = keep.shape[0] // splits
    for i in range(splits):
        here = slice(i * part, (i + 1) * part)
        total[here] = keep[here] + others[i][...]
    for turn in range(n):
        index = share_of(lax.rem(place[0] + turn, n), n)
        at = pl.ds(pl.multiple_of(index * rows, 16), rows)
        outs[turn][...] = total[at, :].astype(outs[turn].dtype)


def halve_kernel(bit, count, place, keep, *refs):
    others, (kept, sent, total) = refs[:count], refs[-3:]
    rows = keep.shape[0] // len(others)
    for i, other in enumerate(others):
        here = slice(i * rows, (i + 1) * rows)
        total[here] = keep[here] + other[...].astype(F32)
    half = kept.shape[0]
    mine = lax.rem(place[0] // bit, 2)
    kept[...] = total[pl.ds(pl.multiple_of(mine * half, 16), half), :]
    sent[...] = total[pl.ds(pl.multiple_of((1 - mine) * half, 16), half), :].astype(BF16)


def back_kernel(sizes, low, own, high, cot, slope, w, back_one, delta):
    members, q, near, far = sizes

    def block(b):
        if b < 0:
            return low[(b + far) * q : (b + far + 1) * q]
        if b >= members:
            return high[(b - members) * q : (b - members + 1) * q]
        return own[b * q : (b + 1) * q]

    for b in range(members):
        here = slice(b * q, (b + 1) * q)
        product = back_dot((block(b + far), block(b), block(b - far)), w, w.shape[0] // 2)
        back = cot[here].astype(F32) + product
        back_one[here] = back
        delta[here] = (back * slope[here]).astype(BF16)


def input_kernel(sizes, place, low, own, high, back_one, w, out):
    members, q, near = sizes
    j = place[1]

    def block(b):
        if b < 0:
            return low[(b + near) * q : (b + near + 1) * q]
        if b >= members:
            return high[(b - members) * q : (b - members + 1) * q]
        return own[b * q : (b + 1) * q]

    for b in range(members):
        here = slice(b * q, (b + 1) * q)
        product = back_dot((block(b + near), block(b), block(b - near)), w, 0)
        value = (back_one[here] + product).astype(BF16)
        out[pl.ds(pl.multiple_of((j ^ b) * q, 16), q), :] = value


def call(kernel, out_shapes, scratch=(), scalars=0, operands=()):
    specs = [SMEM] * scalars + [VMEM] * (len(operands) - scalars)
    return pl.pallas_call(
        kernel,
        out_shape=tuple(jax.ShapeDtypeStruct(shape, kind) for shape, kind in out_shapes),
        in_specs=specs,
        out_specs=tuple(VMEM for _ in out_shapes),
        scratch_shapes=list(scratch),
        cost_estimate=pl.CostEstimate(flops=1, transcendentals=0, bytes_accessed=1),
        compiler_params=pltpu.CompilerParams(vmem_limit_bytes=8 * 1024 * 1024),
    )(*operands)


def core_sum(place, keep, sends, waits):
    n = lax.axis_size("seq")
    others = [swapped(send, "sub", 1) for send in sends]
    if n > 4:
        return [keep + jnp.concatenate(others, 0)]
    shape = (keep.shape[0] // n, keep.shape[1])
    return call(
        functools.partial(share_kernel, n, len(sends)),
        ((shape, F32),) + ((shape, BF16),) * (n - 1),
        scratch=(pltpu.VMEM(keep.shape, F32),),
        scalars=1,
        operands=(place, keep, *others, *waits),
    )


def seq_parts(shares):
    if len(shares) == 1:
        return [lax.psum(shares[0], "seq")]
    return [shares[0]] + [turned(shares[t], "seq", t) for t in range(1, len(shares))]


def halved(place, keep, others, bit, waits=()):
    rows, channels = keep.shape
    shape = (rows // 2, channels)
    return call(
        functools.partial(halve_kernel, bit, len(others)),
        ((shape, F32), (shape, BF16)),
        scratch=(pltpu.VMEM((rows, channels), F32),),
        scalars=1,
        operands=(place, keep, *others, *waits),
    )


def core_sum_halving(place, keep, sends, waits=()):
    others = [swapped(send, "sub", 1) for send in sends]
    n = lax.axis_size("seq")
    if n > 4:
        total = keep + jnp.concatenate(others, 0)
        return total, total
    return halved(place, keep, others, 1, waits)


def first_half(sent):
    return sent if lax.axis_size("seq") > 4 else swapped(sent, "seq", 1)


def seq_sum_halving(place, kept, got, others, waits=()):
    n = lax.axis_size("seq")
    if n > 4:
        return [lax.psum(kept, "seq")]
    bit = 2
    while bit < n:
        came = got if others is None else after(got, others)
        kept, sent = halved(place, kept, [came], bit, waits)
        got = swapped(sent, "seq", bit)
        bit *= 2
    return [kept, got]


def added(pieces):
    total = pieces[0]
    for piece in pieces[1:]:
        total = total + piece.astype(F32)
    return total


def chip_sum(total_one, total_two, j):
    n = lax.axis_size("sub")
    owned = n // 4
    one = total_one.reshape(owned, -1, total_one.shape[1])
    two = total_two.reshape(owned, -1, total_two.shape[1])
    high = j >= n // 2
    part, send = jnp.where(high, two, one), jnp.where(high, one, two)
    part = part + swapped(send.astype(BF16), "sub", n // 2).astype(F32)
    bit = 2
    while bit < n // 2:
        mine = (j & bit) != 0
        keep, send = jnp.where(mine, part[1::2], part[0::2]), jnp.where(mine, part[0::2], part[1::2])
        part = keep + swapped(send.astype(BF16), "sub", bit).astype(F32)
        bit *= 2
    return part[0]


def spread_seq(total, sent, s):
    n = lax.axis_size("seq")
    if n > 4:
        return total
    rows, channels = total.shape
    whole = jnp.zeros((n * rows, channels), F32)
    whole = lax.dynamic_update_slice_in_dim(whole, total, share_of(s, n) * rows, 0)
    for turn in range(1, n):
        got = turned(sent, "seq", turn).astype(F32)
        at = share_of(lax.rem(s + n - turn, n), n) * rows
        whole = lax.dynamic_update_slice_in_dim(whole, got, at, 0)
    return whole


def per_device(activations, cotangent, weights):
    count, channels = activations.shape
    groups, members = lax.axis_size("seq"), lax.axis_size("sub")
    s, j = lax.axis_index("seq"), lax.axis_index("sub")
    place = jnp.stack([s, j]).astype(jnp.int32)
    near, far = DILATION_FIRST // count, DILATION_SECOND // count
    q = count // members
    taps = 3 * channels
    grad_scale = 1.0 / math.sqrt(count * groups * members)

    def kernel(body, *shapes, scratch=(), operands=()):
        return call(body, shapes, scratch, 1, (place,) + tuple(operands))

    def regrouped(block, others=None, first=None):
        pieces = [cut(block, j ^ r, q) for r in range(1, members)]
        if others is not None:
            pieces[1:] = after(pieces[1:], others)
        first = swapped(pieces[0], "sub", 1) if first is None else first
        return [first] + [swapped(piece, "sub", r + 2) for r, piece in enumerate(pieces[1:])]

    reach = near + far
    near_weights = swapped(weights, "sub", 1)
    near_cot = swapped(cut(cotangent, j ^ 1, q), "sub", 1)
    act, up_act, down_act = kernel(
        functools.partial(regroup_kernel, (members, q, reach)),
        ((count, channels), BF16),
        ((reach * q, channels), BF16),
        ((reach * q, channels), BF16),
        operands=(activations, *regrouped(activations), near_weights),
    )
    low, high = shifted(up_act, "seq", 1), shifted(down_act, "seq", -1)
    w_pieces = gather_pieces(weights, near_weights, "sub", act)
    c_pieces = regrouped(cotangent, w_pieces[members // 2], near_cot)

    hidden, slope_one, slope_two, all_weights = kernel(
        functools.partial(forward_kernel, (groups, members, q, near, far)),
        ((count + 2 * far * q, channels), BF16),
        ((count, channels), F32),
        ((count, channels), F32),
        ((2 * taps, channels), BF16),
        operands=(low, act, high, *w_pieces),
    )
    delta_two, up_two, down_two, cot = kernel(
        functools.partial(delta_kernel, (members, q, far)),
        ((count, channels), BF16),
        ((far * q, channels), BF16),
        ((far * q, channels), BF16),
        ((count, channels), BF16),
        operands=(slope_two, cotangent, *c_pieces),
    )
    two_low, two_high = shifted(up_two, "seq", 1), shifted(down_two, "seq", -1)
    splits, more = 4, 2
    half = ((taps // 2, channels), F32)
    share = ((taps // 2 // splits, channels), BF16)
    less = ((taps // 2 // more, channels), BF16)
    keep_two, *send_two = kernel(
        functools.partial(grad_two_kernel, (members, 0, splits, far * q), grad_scale),
        half,
        *[share] * splits,
        operands=(hidden, delta_two),
    )
    kept_two, sent_two = core_sum_halving(place, keep_two, send_two)
    back_one, delta_one = call(
        functools.partial(back_kernel, (members, q, near, far)),
        (((count, channels), F32), ((count, channels), BF16)),
        operands=(two_low, delta_two, two_high, cot, slope_one, all_weights),
    )
    keep_one, *send_one, up_one, down_one = kernel(
        functools.partial(grad_kernel, (members, near * q, more, near * q), grad_scale),
        half,
        *[less] * more,
        ((near * q, channels), BF16),
        ((near * q, channels), BF16),
        operands=(low, act, high, delta_one),
    )
    got_two = first_half(after(sent_two, (two_low, two_high)))
    kept_one, sent_one = core_sum_halving(place, keep_one, send_one, (got_two,))
    got_one = first_half(sent_one)
    up_one, down_one = after((up_one, down_one), sent_one)
    one_low, one_high = shifted(up_one, "seq", 1), shifted(down_one, "seq", -1)
    parts_two = seq_sum_halving(place, kept_two, got_two, sent_one)
    parts_one = seq_sum_halving(place, kept_one, got_one, None, parts_two[1:])

    (grad_in,) = call(
        functools.partial(input_kernel, (members, q, near)),
        (((count, channels), BF16),),
        scalars=1,
        operands=(place, one_low, delta_one, one_high, back_one, all_weights),
    )
    total_one = added(after(parts_one, (one_low, one_high)))
    total_two = added(parts_two)
    part = chip_sum(total_one, total_two, j)
    sent = part.astype(BF16)
    got = [grad_in[r * q : (r + 1) * q] for r in range(members)]
    got = got[:1] + [swapped(got[r], "sub", r) for r in range(1, members)]
    got = after(got, sent)
    input_grad = jnp.zeros((count, channels), BF16)
    for r in range(members):
        input_grad = lax.dynamic_update_slice_in_dim(input_grad, got[r], (j ^ r) * q, 0)

    weight_grad = spread_seq(part, sent, s)
    return (input_grad, weight_grad)


def solution(mesh):
    placed = (P(("grp", "seq", "sub"), None), P(("grp", "seq", "sub"), None), P("sub", None))
    return jax.shard_map(
        per_device,
        mesh=mesh,
        in_specs=placed,
        out_specs=(P(("grp", "seq", "sub"), None), P(("grp", "sub"), None)),
        check_vma=False,
    )
```
